32 devices in a mesh: ens: 2 (over x), lon: 4 (over y, core), lat: 4 (over z).
Axes of the slice: x: 2, y: 2, z: 4, core: 2. Of those that a mesh axis runs over, the one named last changes fastest.
Arguments:
- fields: bfloat16 [8, 768, 1024], P(('ens', 'lat'), 'lon'), parts along dimension 0, may hold values from -6 to 6
- conv_weight: bfloat16 [9216, 1024], P(None, 'lon'), may hold values from -0.0625 to 0.0625
- norm_gain: float32 [1024], replicated, may hold values from 0.1 to 1.9
- qkv_weight: bfloat16 [1024, 3072], replicated, may hold values from -0.1875 to 0.1875
- out_weight: bfloat16 [1024, 1024], replicated, may hold values from -0.1875 to 0.1875
- key_bias: bfloat16 [4, 768, 16], P('lat', 'lon'), may hold values from -8 to 250
Outputs:
- mixed: bfloat16 [8, 768, 1024], P(('ens', 'lat'), 'lon'), parts along dimension 0
The draws below stay inside these ranges and needn't reach their ends.
There are 2 independent parts, one for each index of `ens`. The reference program is written for one: setup_inputs(seed, part) draws one part's arguments, and reference() takes and returns one part's arrays. A program takes and returns all parts, laid end to end along the dimension named above; an argument that names none is the same for every part. Nothing has to cross between parts.
All inputs are finite; a program needn't handle non-finite values.
Results may differ from the reference program's by a relative error of at most 0.012.
Values may be sent and summed in bfloat16 or wider, within the bound.
No kernel may reach another device: no remote copies, remote signals or barrier semaphores. Data moves between devices by JAX's collectives and lax.ppermute only.
A program may use at most 128 MiB of HBM per device.

```python
import jax
import jax.numpy as jnp
from jax import lax

D = 1024
H = 16
NLAT = 4
NLON = 768


def draw_key_bias(key, part):
    first = jax.random.fold_in(key, 0)
    values = jnp.clip(2.0 * jax.random.normal(first, (NLAT, NLON, H), jnp.float32), -8.0, 8.0)
    return values.astype(jnp.bfloat16)


def shard_levels(own_key, shape, pieces, smallest, largest):
    factor_of = 1.0
    for position, parts in pieces:
        steps = jax.random.uniform(jax.random.fold_in(jax.random.fold_in(own_key, 6), position), (parts,), jnp.float32, smallest / len(pieces), largest / len(pieces))
        factor_of = factor_of * jnp.repeat(jnp.exp(steps), shape[position] // parts).reshape((-1,) + (1,) * (len(shape) - 1 - position))
    return factor_of


def centred(key, extent, scale, most, shards=(), kind=jnp.bfloat16):
    factor_of = shard_levels(key, extent, shards, -0.22, 0.18) if shards else 1.0
    drawn = jax.random.normal(key, extent, jnp.float32) * scale * factor_of
    return jnp.minimum(jnp.maximum(drawn, -most), most).astype(kind)


def setup_inputs(seed: int = 0, part: int = 0) -> dict:
    key_list = jax.random.split(jax.random.key(seed), 7)
    own_keys = jax.random.split(jax.random.fold_in(key_list[6], part), 7)
    fields = centred(own_keys[0], (NLAT, NLON, D), 1.0, 6.0, ((0, 4), (1, 4)))
    conv_weight = centred(key_list[1], (9 * D, D), (9 * D) ** -0.5, 0.0625, ((1, 4),))
    norm_gain = jnp.clip(1.0 + 0.18 * jax.random.normal(key_list[2], (D,), jnp.float32), 0.1, 1.9)
    qkv_weight = centred(key_list[3], (D, 3 * D), D ** -0.5, 0.1875)
    out_weight = centred(key_list[4], (D, D), D ** -0.5, 0.1875)
    key_bias = draw_key_bias(jax.random.fold_in(key_list[6], 71), part)
    return dict(fields=fields, conv_weight=conv_weight, norm_gain=norm_gain, qkv_weight=qkv_weight, out_weight=out_weight, key_bias=key_bias)


def one_row(row_parts):
    query_row, key_row, value_row, bias_row = row_parts
    head_dim = D // H
    query_heads = query_row.reshape(NLON, H, head_dim).astype(jnp.float32)
    key_heads = key_row.reshape(NLON, H, head_dim).astype(jnp.float32)
    value_heads = value_row.reshape(NLON, H, head_dim).astype(jnp.float32)
    scores = jnp.einsum('qhd,khd->hqk', query_heads, key_heads) / jnp.sqrt(jnp.float32(head_dim))
    scores = scores + jnp.transpose(bias_row.astype(jnp.float32))[:, None, :]
    best = lax.optimization_barrier(jnp.max(scores, axis=-1, keepdims=True))
    weights = jnp.exp(scores - best)
    totals = lax.optimization_barrier(jnp.sum(weights, axis=-1))
    rounded = weights.astype(jnp.bfloat16).astype(jnp.float32)
    summed = jnp.einsum('hqk,khd->qhd', rounded, value_heads)
    result = summed / jnp.transpose(totals)[:, :, None]
    return result.reshape(NLON, D).astype(jnp.bfloat16)

def reference(fields, conv_weight, norm_gain, qkv_weight, out_weight, key_bias):
    banded = jnp.pad(fields, ((1, 1), (0, 0), (0, 0)))
    wrapped = jnp.concatenate([banded[:, -1:], banded, banded[:, :1]], axis=1)
    accum = jnp.zeros((NLAT * NLON, D), jnp.float32)
    tap_idx = 0
    for step_lat in (-1, 0, 1):
        for step_lon in (-1, 0, 1):
            shifted = wrapped[1 + step_lat:1 + step_lat + NLAT, 1 + step_lon:1 + step_lon + NLON].reshape(NLAT * NLON, D)
            accum = accum + jnp.dot(shifted, conv_weight[tap_idx * D:(tap_idx + 1) * D], preferred_element_type=jnp.float32)
            tap_idx += 1
    conv_out = accum.astype(jnp.bfloat16)
    residual = (fields.reshape(NLAT * NLON, D).astype(jnp.float32) + conv_out.astype(jnp.float32)).astype(jnp.bfloat16)
    stream = residual.astype(jnp.float32)
    normed = (stream * lax.rsqrt(lax.optimization_barrier(jnp.mean(stream * stream, axis=-1, keepdims=True)) + 1e-06) * norm_gain).astype(jnp.bfloat16)
    projected = jnp.dot(normed, qkv_weight, preferred_element_type=jnp.float32).astype(jnp.bfloat16)
    queries = projected[:, :D].reshape(NLAT, NLON, D)
    key_rows = projected[:, D:2 * D].reshape(NLAT, NLON, D)
    value_rows = projected[:, 2 * D:].reshape(NLAT, NLON, D)
    attended = lax.map(one_row, (queries, key_rows, value_rows, key_bias))
    mixed = residual.astype(jnp.float32) + jnp.dot(attended.reshape(NLAT * NLON, D), out_weight, preferred_element_type=jnp.float32)
    return mixed.astype(jnp.bfloat16).reshape(NLAT, NLON, D)
```

```python
import functools
import math

import jax
import jax.numpy as jnp
from jax import lax
from jax.experimental import pallas as pl
from jax.experimental.pallas import tpu as pltpu
from jax.sharding import PartitionSpec as P

H = 16
EDGE = 16
F32 = jnp.float32
BF16 = jnp.bfloat16


def extended(block, sides, width):
    for axis, dim in sides:
        count = lax.axis_size(axis)
        forward = [(i, i + 1) for i in range(count - 1)]
        backward = [(target, source) for source, target in forward]
        low = lax.ppermute(
            lax.slice_in_dim(block, block.shape[dim] - width, None, axis=dim), axis, forward
        )
        high = lax.ppermute(lax.slice_in_dim(block, 0, width, axis=dim), axis, backward)
        block = jnp.concatenate([low, block, high], axis=dim)
    return block


def tap_sum(wrapped, conv_weight, out_rows, lon_total, channels):
    out_width = conv_weight.shape[1]
    accum_cols = jnp.zeros((out_rows * lon_total, out_width), jnp.float32)
    tap_idx = 0
    for step_lat in (-1, 0, 1):
        for step_lon in (-1, 0, 1):
            shifted = wrapped[
                1 + step_lat : 1 + step_lat + out_rows, 1 + step_lon : 1 + step_lon + lon_total
            ].reshape(out_rows * lon_total, channels)
            accum_cols = accum_cols + jnp.dot(
                shifted,
                conv_weight[tap_idx * channels : (tap_idx + 1) * channels],
                preferred_element_type=jnp.float32,
            )
            tap_idx += 1
    return accum_cols.reshape(out_rows, lon_total, out_width)


def general_device(fields, conv_weight, norm_gain, qkv_weight, out_weight, key_bias):
    lat_n, lon_n, channels = fields.shape
    row_count = lat_n * lon_n
    head_dim = channels // H
    score_scale = 1.0 / math.sqrt(head_dim)
    banded = extended(fields, (("lat", 0),), 1)
    circle = lax.all_gather(banded, "lon", axis=1, tiled=True)
    lon_total = circle.shape[1]
    wrapped = jnp.concatenate([circle[:, -1:], circle, circle[:, :1]], axis=1)
    out_cols = tap_sum(wrapped, conv_weight, lat_n, lon_total, channels).astype(jnp.bfloat16)
    conv_out = lax.all_to_all(out_cols, "lon", split_axis=1, concat_axis=2, tiled=True).reshape(
        row_count, channels
    )
    residual = (
        fields.reshape(row_count, channels).astype(jnp.float32) + conv_out.astype(jnp.float32)
    ).astype(jnp.bfloat16)
    stream = residual.astype(jnp.float32)
    normed = (
        stream * lax.rsqrt(jnp.mean(stream * stream, axis=-1, keepdims=True) + 1e-06) * norm_gain
    ).astype(jnp.bfloat16)
    projected = jnp.dot(normed, qkv_weight, preferred_element_type=jnp.float32).astype(jnp.bfloat16)
    queries = projected[:, :channels].reshape(lat_n, lon_n, channels)
    key_rows = projected[:, channels : 2 * channels].reshape(lat_n, lon_n, channels)
    value_rows = projected[:, 2 * channels :].reshape(lat_n, lon_n, channels)
    query_heads = queries.reshape(lat_n, lon_n, H, head_dim)
    key_part = lax.all_gather(key_rows, "lon", axis=1, tiled=True)
    value_part = lax.all_gather(value_rows, "lon", axis=1, tiled=True)
    bias_part = lax.all_gather(key_bias, "lon", axis=1, tiled=True)
    span = key_part.shape[1]
    key_heads = key_part.reshape(lat_n, span, H, head_dim)
    value_heads = value_part.reshape(lat_n, span, H, head_dim)
    scores = (
        jnp.einsum("aqhd,akhd->ahqk", query_heads, key_heads, preferred_element_type=jnp.float32)
        * score_scale
    )
    scores = scores + jnp.transpose(bias_part, (0, 2, 1)).astype(jnp.float32)[:, :, None, :]
    weights = jnp.exp(scores - jnp.max(scores, axis=-1)[..., None])
    denom = jnp.sum(weights, axis=-1)
    accum = jnp.einsum(
        "ahqk,akhd->ahqd",
        weights.astype(jnp.bfloat16),
        value_heads,
        preferred_element_type=jnp.float32,
    )
    attended = (
        jnp.transpose(accum / denom[..., None], (0, 2, 1, 3))
        .reshape(row_count, channels)
        .astype(jnp.bfloat16)
    )
    mixed = residual.astype(jnp.float32) + jnp.dot(
        attended, out_weight, preferred_element_type=jnp.float32
    )
    return mixed.astype(jnp.bfloat16).reshape(lat_n, lon_n, channels)


VMEM = pltpu.VMEM
ANY = pl.ANY


def vspec():
    return pl.BlockSpec(memory_space=VMEM)


def sspec():
    return pl.BlockSpec(memory_space=pltpu.SMEM)


def aspec():
    return pl.BlockSpec(memory_space=ANY)


def conv_kernel(me, xa, xb, ea, eb, w_any, up, down, mid, ext, cols, wbuf, sem):
    n, ch = xa.shape
    copies = []
    for a in range(3):
        copy = pltpu.make_async_copy(w_any.at[pl.ds(a * 3 * ch, 3 * ch)], wbuf.at[a], sem.at[a])
        copy.start()
        copies.append(copy)
    core = me[0] % 2
    ext[pl.ds(pl.multiple_of(EDGE + core * n, 16), n), :] = xa[...]
    ext[pl.ds(pl.multiple_of(EDGE + (1 - core) * n, 16), n), :] = xb[...]
    far = EDGE + 2 * n
    ext[pl.ds(pl.multiple_of((1 - core) * far, 16), EDGE), :] = ea[...]
    ext[pl.ds(pl.multiple_of(core * far, 16), EDGE), :] = eb[...]
    for b in range(3):
        cols[:, b * ch : (b + 1) * ch] = ext[EDGE - 1 + b : EDGE - 1 + b + 2 * n, :]
    for a, out in ((0, up), (2, down), (1, mid)):
        copies[a].wait()
        out[...] = jnp.dot(cols[...], wbuf[a], preferred_element_type=F32).astype(out.dtype)


def conv_half(me, xa, xb, ea, eb, w):
    n, ch = xa.shape
    width = w.shape[1]
    return pl.pallas_call(
        conv_kernel,
        out_shape=(
            jax.ShapeDtypeStruct((2 * n, width), BF16),
            jax.ShapeDtypeStruct((2 * n, width), BF16),
            jax.ShapeDtypeStruct((2 * n, width), F32),
        ),
        in_specs=[sspec()] + [vspec()] * 4 + [aspec()],
        out_specs=(vspec(),) * 3,
        scratch_shapes=[
            VMEM((2 * n + 2 * EDGE, ch), BF16),
            VMEM((2 * n, 3 * ch), BF16),
            VMEM((3, 3 * ch, width), BF16),
            pltpu.SemaphoreType.DMA((3,)),
        ],
        compiler_params=pltpu.CompilerParams(vmem_limit_bytes=20 << 20),
        cost_estimate=pl.CostEstimate(
            flops=2 * 2 * n * 9 * ch * width, bytes_accessed=2 * 9 * ch * width, transcendentals=0
        ),
        name="conv_half",
    )(me, xa, xb, ea, eb, w)


def normed_of(blocks, gain, lane, ch):
    width = blocks[0].shape[1]
    streams = [b[...].astype(F32) for b in blocks]
    square = sum(jnp.sum(s * s, axis=-1, keepdims=True) for s in streams)
    factor = lax.rsqrt(square * (1.0 / ch) + 1e-06)
    return [(s * factor * gain[lane ^ k]).astype(BF16) for k, s in enumerate(streams)]


def keys_kernel(me, b0, b1, b2, b3, gain, w, k_out, v_out):
    lane = me[0]
    rows, width = b0.shape
    ch = w.shape[0]
    parts = normed_of((b0, b1, b2, b3), gain, lane, ch)
    for out, first in ((k_out, ch), (v_out, 2 * ch)):
        acc = None
        for k, part in enumerate(parts):
            at = pl.multiple_of((lane ^ k) * width, width)
            term = jnp.dot(part, w[pl.ds(at, width), first : first + ch], preferred_element_type=F32)
            acc = term if acc is None else acc + term
        out[...] = acc.astype(BF16)


def keys_of(me, blocks, gain, w):
    rows, width = blocks[0].shape
    ch = w.shape[0]
    out = jax.ShapeDtypeStruct((rows, ch), BF16)
    return pl.pallas_call(
        keys_kernel,
        out_shape=(out, out),
        in_specs=[sspec()] + [vspec()] * 6,
        out_specs=(vspec(), vspec()),
        compiler_params=pltpu.CompilerParams(vmem_limit_bytes=24 << 20),
        cost_estimate=pl.CostEstimate(
            flops=2 * rows * ch * 2 * ch, bytes_accessed=4 * ch * ch, transcendentals=0
        ),
        name="keys_of",
    )(me, *blocks, gain, w)


def attend_kernel(
    me, b0, b1, b2, b3, gain, w, k_far, v_far, bias, w_out, out, keys, values, query, attended
):
    lane = me[0]
    core = lane % 2
    rows, width = b0.shape
    n = rows // 2
    ch = w.shape[0]
    hd = ch // H
    blocks = (b0, b1, b2, b3)
    parts = normed_of(blocks, gain, lane, ch)
    for first, dst in ((ch, keys), (2 * ch, values), (0, query)):
        acc = None
        for k, part in enumerate(parts):
            at = pl.multiple_of((lane ^ k) * width, width)
            term = jnp.dot(part, w[pl.ds(at, width), first : first + ch], preferred_element_type=F32)
            acc = term if acc is None else acc + term
        dst[0:rows, :] = acc.astype(BF16)
    keys[rows : 2 * rows, :] = k_far[...]
    values[rows : 2 * rows, :] = v_far[...]
    own = pl.multiple_of(core * n, 16)
    group = 256 // hd
    head_of = lax.broadcasted_iota(jnp.int32, (n, 256), 1) // hd
    for g in range(ch // 256):
        cols = slice(g * 256, (g + 1) * 256)
        q = query[pl.ds(own, n), cols] * jnp.asarray(1.0 / math.sqrt(hd), BF16)
        stacked = jnp.concatenate(
            [jnp.where(head_of == t, q, jnp.zeros_like(q)) for t in range(group)], axis=0
        )
        scores = lax.dot_general(
            stacked, keys[:, cols], (((1,), (1,)), ((), ())), preferred_element_type=F32
        )
        values_g = values[:, cols]
        result = jnp.zeros((n, 256), F32)
        for t in range(group):
            head = g * group + t
            s = scores[t * n : (t + 1) * n] + bias[head : head + 1, :]
            e = jnp.exp(s - jnp.max(s, axis=-1, keepdims=True))
            total = jnp.sum(e, axis=-1, keepdims=True)
            o = jnp.dot(e.astype(BF16), values_g, preferred_element_type=F32)
            result = jnp.where(head_of == t, o / total, result)
        attended[:, cols] = result.astype(BF16)
    for k, block in enumerate(blocks):
        at = pl.multiple_of((lane ^ k) * width, width)
        mixed = block[pl.ds(own, n), :].astype(F32) + jnp.dot(
            attended[...], w_out[:, pl.ds(at, width)], preferred_element_type=F32
        )
        out[:, pl.ds(at, width)] = mixed.astype(BF16)


def attend(me, blocks, gain, w, k_far, v_far, bias, w_out):
    rows, width = blocks[0].shape
    n = rows // 2
    ch = w.shape[0]
    return pl.pallas_call(
        attend_kernel,
        out_shape=jax.ShapeDtypeStruct((n, ch), BF16),
        in_specs=[sspec()] + [vspec()] * 10,
        out_specs=vspec(),
        scratch_shapes=[
            VMEM((2 * rows, ch), BF16),
            VMEM((2 * rows, ch), BF16),
            VMEM((rows, ch), BF16),
            VMEM((n, ch), BF16),
        ],
        compiler_params=pltpu.CompilerParams(vmem_limit_bytes=40 << 20),
        cost_estimate=pl.CostEstimate(
            flops=2 * rows * ch * 3 * ch + 4 * n * 2 * rows * ch * 4,
            bytes_accessed=8 * ch * ch,
            transcendentals=n * 2 * rows * H,
        ),
        name="attend",
    )(me, *blocks, gain, w, k_far, v_far, bias, w_out)


def four_shard_device(fields, conv_weight, norm_gain, qkv_weight, out_weight, key_bias):
    lat_n, n, ch = fields.shape
    width = conv_weight.shape[1]
    lane = lax.axis_index("lon")
    core = lane % 2
    me = jnp.reshape(lane, (1,)).astype(jnp.int32)
    lon_size = lax.axis_size("lon")
    lat_size = lax.axis_size("lat")

    def swap(value, bit):
        return lax.ppermute(value, "lon", [(i, i ^ bit) for i in range(lon_size)])

    def north(value):
        return lax.ppermute(value, "lat", [(i, i + 1) for i in range(lat_size - 1)])

    def south(value):
        return lax.ppermute(value, "lat", [(i + 1, i) for i in range(lat_size - 1)])

    x = fields.reshape(n, ch)
    edge = lax.dynamic_slice_in_dim(x, core * (n - EDGE), EDGE, axis=0)
    edge_y = swap(edge, 2)
    edge_d = swap(edge_y, 1)
    x_c = swap(x, 1)
    x_y = swap(x, 2)
    x_d = swap(x_y, 1)
    edge_c = lax.dynamic_slice_in_dim(x_c, (1 - core) * (n - EDGE), EDGE, axis=0)
    b = key_bias.reshape(n, H)
    b_c = swap(b, 1)
    b_y = swap(b, 2)
    b_d = swap(b_y, 1)

    def in_order(a, c):
        return jnp.where(core == 0, jnp.concatenate([a, c]), jnp.concatenate([c, a]))

    bias = jnp.concatenate([in_order(b, b_c), in_order(b_y, b_d)]).astype(F32).T

    up1, down1, mid1 = conv_half(me, x, x_c, edge_y, edge_d, conv_weight)
    up1, down1 = north(up1), south(down1)
    up2, down2, mid2 = conv_half(me, x_y, x_d, edge, edge_c, conv_weight)
    up2, down2 = north(up2), south(down2)

    def residual_of(up, down, mid, xa, xb):
        conv_out = (up.astype(F32) + down.astype(F32) + mid).astype(BF16)
        cols = lambda v: lax.dynamic_slice_in_dim(v, lane * width, width, axis=1)
        return (in_order(cols(xa), cols(xb)).astype(F32) + conv_out.astype(F32)).astype(BF16)

    near = residual_of(up1, down1, mid1, x, x_c)
    near_c = swap(near, 1)
    far_y = swap(near, 2)
    far_d = swap(far_y, 1)
    far = residual_of(up2, down2, mid2, x_y, x_d)
    far_c = swap(far, 1)
    near_y = swap(far, 2)
    near_d = swap(near_y, 1)
    gain = norm_gain.reshape(lon_size, 1, width)
    k_far, v_far = keys_of(me, (far, far_c, far_y, far_d), gain, qkv_weight)
    out = attend(
        me, (near, near_c, near_y, near_d), gain, qkv_weight, k_far, v_far, bias, out_weight
    )
    return out.reshape(fields.shape)


def solution(mesh):
    def on_device(*args):
        fields, conv_weight = args[0], args[1]
        special = (
            mesh.shape["lon"] == 4
            and fields.shape[0] == 1
            and conv_weight.shape[1] % 256 == 0
            and fields.shape[1] % 32 == 0
        )
        return (four_shard_device if special else general_device)(*args)

    return jax.shard_map(
        on_device,
        mesh=mesh,
        in_specs=(
            P(("ens", "lat"), "lon", None),
            P(None, "lon"),
            P(),
            P(),
            P(),
            P("lat", "lon", None),
        ),
        out_specs=P(("ens", "lat"), "lon", None),
        check_vma=False,
    )
```

```python
import math

import jax
import jax.numpy as jnp
from jax import lax
from jax.experimental import pallas as pl
from jax.experimental.pallas import tpu as pltpu
from jax.sharding import PartitionSpec as P


H = 16
EDGE = 16
PIECES = 8
F32 = jnp.float32
BF16 = jnp.bfloat16


def extended(block, sides, width):
    for axis, dim in sides:
        count = lax.axis_size(axis)
        forward = [(i, i + 1) for i in range(count - 1)]
        backward = [(target, source) for source, target in forward]
        low = lax.ppermute(
            lax.slice_in_dim(block, block.shape[dim] - width, None, axis=dim), axis, forward
        )
        high = lax.ppermute(lax.slice_in_dim(block, 0, width, axis=dim), axis, backward)
        block = jnp.concatenate([low, block, high], axis=dim)
    return block


def tap_sum(wrapped, conv_weight, out_rows, lon_total, channels):
    out_width = conv_weight.shape[1]
    accum_cols = jnp.zeros((out_rows * lon_total, out_width), jnp.float32)
    tap_idx = 0
    for step_lat in (-1, 0, 1):
        for step_lon in (-1, 0, 1):
            shifted = wrapped[
                1 + step_lat : 1 + step_lat + out_rows, 1 + step_lon : 1 + step_lon + lon_total
            ].reshape(out_rows * lon_total, channels)
            accum_cols = accum_cols + jnp.dot(
                shifted,
                conv_weight[tap_idx * channels : (tap_idx + 1) * channels],
                preferred_element_type=jnp.float32,
            )
            tap_idx += 1
    return accum_cols.reshape(out_rows, lon_total, out_width)


def general_device(fields, conv_weight, norm_gain, qkv_weight, out_weight, key_bias):
    lat_n, lon_n, channels = fields.shape
    row_count = lat_n * lon_n
    head_dim = channels // H
    score_scale = 1.0 / math.sqrt(head_dim)
    banded = extended(fields, (("lat", 0),), 1)
    circle = lax.all_gather(banded, "lon", axis=1, tiled=True)
    lon_total = circle.shape[1]
    wrapped = jnp.concatenate([circle[:, -1:], circle, circle[:, :1]], axis=1)
    out_cols = tap_sum(wrapped, conv_weight, lat_n, lon_total, channels).astype(jnp.bfloat16)
    conv_out = lax.all_to_all(out_cols, "lon", split_axis=1, concat_axis=2, tiled=True).reshape(
        row_count, channels
    )
    residual = (
        fields.reshape(row_count, channels).astype(jnp.float32) + conv_out.astype(jnp.float32)
    ).astype(jnp.bfloat16)
    stream = residual.astype(jnp.float32)
    normed = (
        stream * lax.rsqrt(jnp.mean(stream * stream, axis=-1, keepdims=True) + 1e-06) * norm_gain
    ).astype(jnp.bfloat16)
    projected = jnp.dot(normed, qkv_weight, preferred_element_type=jnp.float32).astype(jnp.bfloat16)
    queries = projected[:, :channels].reshape(lat_n, lon_n, channels)
    key_rows = projected[:, channels : 2 * channels].reshape(lat_n, lon_n, channels)
    value_rows = projected[:, 2 * channels :].reshape(lat_n, lon_n, channels)
    query_heads = queries.reshape(lat_n, lon_n, H, head_dim)
    key_part = lax.all_gather(key_rows, "lon", axis=1, tiled=True)
    value_part = lax.all_gather(value_rows, "lon", axis=1, tiled=True)
    bias_part = lax.all_gather(key_bias, "lon", axis=1, tiled=True)
    span = key_part.shape[1]
    key_heads = key_part.reshape(lat_n, span, H, head_dim)
    value_heads = value_part.reshape(lat_n, span, H, head_dim)
    scores = (
        jnp.einsum("aqhd,akhd->ahqk", query_heads, key_heads, preferred_element_type=jnp.float32)
        * score_scale
    )
    scores = scores + jnp.transpose(bias_part, (0, 2, 1)).astype(jnp.float32)[:, :, None, :]
    weights = jnp.exp(scores - jnp.max(scores, axis=-1)[..., None])
    denom = jnp.sum(weights, axis=-1)
    accum = jnp.einsum(
        "ahqk,akhd->ahqd",
        weights.astype(jnp.bfloat16),
        value_heads,
        preferred_element_type=jnp.float32,
    )
    attended = (
        jnp.transpose(accum / denom[..., None], (0, 2, 1, 3))
        .reshape(row_count, channels)
        .astype(jnp.bfloat16)
    )
    mixed = residual.astype(jnp.float32) + jnp.dot(
        attended, out_weight, preferred_element_type=jnp.float32
    )
    return mixed.astype(jnp.bfloat16).reshape(lat_n, lon_n, channels)


VMEM = pltpu.VMEM
ANY = pl.ANY


def vspec():
    return pl.BlockSpec(memory_space=VMEM)


def sspec():
    return pl.BlockSpec(memory_space=pltpu.SMEM)


def aspec():
    return pl.BlockSpec(memory_space=ANY)


def vout(shape, dtype):
    return VMEM(shape, dtype)


def load_kernel(*refs):
    count = (len(refs) - 1) // 2
    sem = refs[-1]
    copies = []
    for src, dst in zip(refs[:count], refs[count : 2 * count]):
        rows = src.shape[0]
        pieces = PIECES if rows % (16 * PIECES) == 0 else 1
        size = rows // pieces
        for p in range(pieces):
            at = pl.ds(p * size, size)
            copy = pltpu.make_async_copy(src.at[at], dst.at[at], sem.at[len(copies)])
            copy.start()
            copies.append(copy)
    for copy in copies:
        copy.wait()


def load(*arrays):
    total = sum(a.size * a.dtype.itemsize for a in arrays)
    return pl.pallas_call(
        load_kernel,
        out_shape=tuple(vout(a.shape, a.dtype) for a in arrays),
        in_specs=[aspec()] * len(arrays),
        out_specs=tuple(vspec() for _ in arrays),
        scratch_shapes=[pltpu.SemaphoreType.DMA((PIECES * len(arrays),))],
        compiler_params=pltpu.CompilerParams(vmem_limit_bytes=1 << 20),
        cost_estimate=pl.CostEstimate(flops=0, bytes_accessed=total, transcendentals=0),
        name="load",
    )(*[pltpu.with_memory_space_constraint(a, pltpu.HBM) for a in arrays])


def conv_kernel(me, xa, xb, ea, eb, w, first, second, mid, ext, cols):
    n, ch = xa.shape
    core = me[0] % 2
    if ea.shape[0] == EDGE:
        edge_a, edge_b = ea[...], eb[...]
    else:
        edge_a = ea[pl.ds(pl.multiple_of(core * (n - EDGE), 16), EDGE), :]
        edge_b = eb[pl.ds(pl.multiple_of((1 - core) * (n - EDGE), 16), EDGE), :]
    odd = me[1] % 2
    ext[pl.ds(pl.multiple_of(EDGE + core * n, 16), n), :] = xa[...]
    ext[pl.ds(pl.multiple_of(EDGE + (1 - core) * n, 16), n), :] = xb[...]
    far = EDGE + 2 * n
    ext[pl.ds(pl.multiple_of((1 - core) * far, 16), EDGE), :] = edge_a
    ext[pl.ds(pl.multiple_of(core * far, 16), EDGE), :] = edge_b
    for b in range(3):
        cols[:, b * ch : (b + 1) * ch] = ext[EDGE - 1 + b : EDGE - 1 + b + 2 * n, :]
    for a, out in ((2 * odd, first), (2 - 2 * odd, second), (1, mid)):
        taps = w[pl.ds(pl.multiple_of(a * 3 * ch, 16), 3 * ch), :]
        out[...] = jnp.dot(cols[...], taps, preferred_element_type=F32).astype(out.dtype)


def conv_half(me, xa, xb, ea, eb, w):
    n, ch = xa.shape
    width = w.shape[1]
    return pl.pallas_call(
        conv_kernel,
        out_shape=(
            vout((2 * n, width), BF16),
            vout((2 * n, width), BF16),
            vout((2 * n, width), F32),
        ),
        in_specs=[sspec()] + [vspec()] * 5,
        out_specs=(vspec(),) * 3,
        scratch_shapes=[
            VMEM((2 * n + 2 * EDGE, ch), BF16),
            VMEM((2 * n, 3 * ch), BF16),
        ],
        compiler_params=pltpu.CompilerParams(vmem_limit_bytes=12 << 20),
        cost_estimate=pl.CostEstimate(
            flops=2 * 2 * n * 9 * ch * width, bytes_accessed=2 * 9 * ch * width, transcendentals=0
        ),
        name="conv_half",
    )(me, xa, xb, ea, eb, w)


def residual_kernel(me, first, second, mid, xa, xb, *rest):
    out = rest[-1]
    n = xa.shape[0]
    width = mid.shape[1]
    lane = me[0]
    core = lane % 2
    at = pl.ds(pl.multiple_of(lane * width, width), width)
    for x, place in ((xa, core), (xb, 1 - core)):
        rows = pl.ds(pl.multiple_of(place * n, 16), n)
        conv_out = first[rows, :].astype(F32) + second[rows, :].astype(F32) + mid[rows, :]
        out[rows, :] = (x[:, at].astype(F32) + conv_out.astype(BF16).astype(F32)).astype(BF16)
    if len(rest) == 2:
        out[2 * n : 2 * n + H, :] = rest[0][...]


def residual_of(me, first, second, mid, xa, xb, *extra):
    rows, width = mid.shape
    rows += H * len(extra)
    return pl.pallas_call(
        residual_kernel,
        out_shape=vout((rows, width), BF16),
        in_specs=[sspec()] + [vspec()] * (5 + len(extra)),
        out_specs=vspec(),
        compiler_params=pltpu.CompilerParams(vmem_limit_bytes=4 << 20),
        cost_estimate=pl.CostEstimate(
            flops=4 * rows * width, bytes_accessed=8 * rows * width, transcendentals=0
        ),
        name="residual_of",
    )(me, first, second, mid, xa, xb, *extra)


def normed_of(blocks, gain, lane, ch, rows):
    streams = [b[0:rows, :].astype(F32) for b in blocks]
    square = sum(jnp.sum(s * s, axis=-1, keepdims=True) for s in streams)
    factor = lax.rsqrt(square * (1.0 / ch) + 1e-06)
    return [(s * factor * gain[lane ^ k]).astype(BF16) for k, s in enumerate(streams)]


def keys_kernel(me, b0, b1, b2, b3, gain, w, k_out, v_out):
    lane = me[0]
    rows, ch = k_out.shape
    width = b0.shape[1]
    parts = normed_of((b0, b1, b2, b3), gain, lane, ch, rows)
    for out, first in ((k_out, ch), (v_out, 2 * ch)):
        acc = None
        for k, part in enumerate(parts):
            at = pl.multiple_of((lane ^ k) * width, width)
            term = jnp.dot(part, w[pl.ds(at, width), first : first + ch], preferred_element_type=F32)
            acc = term if acc is None else acc + term
        out[...] = acc.astype(BF16)


def keys_of(me, blocks, gain, w):
    rows = blocks[0].shape[0]
    ch = w.shape[0]
    out = vout((rows, ch), BF16)
    return pl.pallas_call(
        keys_kernel,
        out_shape=(out, out),
        in_specs=[sspec()] + [vspec()] * 6,
        out_specs=(vspec(), vspec()),
        compiler_params=pltpu.CompilerParams(vmem_limit_bytes=24 << 20),
        cost_estimate=pl.CostEstimate(
            flops=2 * rows * ch * 2 * ch, bytes_accessed=4 * ch * ch, transcendentals=0
        ),
        name="keys_of",
    )(me, *blocks, gain, w)


def attend_kernel(
    me, b0, b1, b2, b3, gain, w, k_far, v_far, bias_y, bias_d, w_out, out, keys, values, query, attended
):
    lane = me[0]
    core = lane % 2
    n, ch = out.shape
    rows = 2 * n
    width = b0.shape[1]
    hd = ch // H
    blocks = (b0, b1, b2, b3)
    parts = normed_of(blocks, gain, lane, ch, rows)
    for first, dst in ((ch, keys), (2 * ch, values), (0, query)):
        acc = None
        for k, part in enumerate(parts):
            at = pl.multiple_of((lane ^ k) * width, width)
            term = jnp.dot(part, w[pl.ds(at, width), first : first + ch], preferred_element_type=F32)
            acc = term if acc is None else acc + term
        dst[0:rows, :] = acc.astype(BF16)
    keys[rows : 2 * rows, :] = k_far[...]
    values[rows : 2 * rows, :] = v_far[...]
    pieces = []
    for a, c in ((b0, b1), (bias_y, bias_d)):
        a, c = (v[rows : rows + H, 0:n].astype(F32) for v in (a, c))
        pieces += [jnp.where(core == 0, a, c), jnp.where(core == 0, c, a)]
    bias = jnp.concatenate(pieces, axis=1)
    own = pl.multiple_of(core * n, 16)
    group = 256 // hd
    head_of = lax.broadcasted_iota(jnp.int32, (n, 256), 1) // hd
    for g in range(ch // 256):
        cols = slice(g * 256, (g + 1) * 256)
        q = query[pl.ds(own, n), cols] * jnp.asarray(1.0 / math.sqrt(hd), BF16)
        stacked = jnp.concatenate(
            [jnp.where(head_of == t, q, jnp.zeros_like(q)) for t in range(group)], axis=0
        )
        scores = lax.dot_general(
            stacked, keys[:, cols], (((1,), (1,)), ((), ())), preferred_element_type=F32
        )
        values_g = values[:, cols]
        result = jnp.zeros((n, 256), F32)
        for t in range(group):
            head = g * group + t
            s = scores[t * n : (t + 1) * n] + bias[head : head + 1, :]
            e = jnp.exp(s - jnp.max(s, axis=-1, keepdims=True))
            total = jnp.sum(e, axis=-1, keepdims=True)
            o = jnp.dot(e.astype(BF16), values_g, preferred_element_type=F32)
            result = jnp.where(head_of == t, o / total, result)
        attended[:, cols] = result.astype(BF16)
    for k, block in enumerate(blocks):
        at = pl.multiple_of((lane ^ k) * width, width)
        mixed = block[pl.ds(own, n), :].astype(F32) + jnp.dot(
            attended[...], w_out[:, pl.ds(at, width)], preferred_element_type=F32
        )
        out[:, pl.ds(at, width)] = mixed.astype(BF16)


def attend(me, blocks, gain, w, k_far, v_far, bias_y, bias_d, w_out):
    rows, ch = k_far.shape
    n = rows // 2
    return pl.pallas_call(
        attend_kernel,
        out_shape=jax.ShapeDtypeStruct((n, ch), BF16),
        in_specs=[sspec()] + [vspec()] * 11,
        out_specs=vspec(),
        scratch_shapes=[
            VMEM((2 * rows, ch), BF16),
            VMEM((2 * rows, ch), BF16),
            VMEM((rows, ch), BF16),
            VMEM((n, ch), BF16),
        ],
        compiler_params=pltpu.CompilerParams(vmem_limit_bytes=40 << 20),
        cost_estimate=pl.CostEstimate(
            flops=2 * rows * ch * 3 * ch + 4 * n * 2 * rows * ch * 4,
            bytes_accessed=8 * ch * ch,
            transcendentals=n * 2 * rows * H,
        ),
        name="attend",
    )(me, *blocks, gain, w, k_far, v_far, bias_y, bias_d, w_out)


def four_shard_device(fields, conv_weight, norm_gain, qkv_weight, out_weight, key_bias):
    _, n, ch = fields.shape
    width = conv_weight.shape[1]
    lane = lax.axis_index("lon")
    core = lane % 2
    me = jnp.stack([lane, lax.axis_index("lat")]).astype(jnp.int32)
    lon_size = lax.axis_size("lon")
    lat_size = lax.axis_size("lat")

    def swap(value, bit):
        return lax.ppermute(value, "lon", [(i, i ^ bit) for i in range(lon_size)])

    def lat_swap(value, first):
        pairs = [(i, i + 1) for i in range(first, lat_size - 1, 2)]
        return lax.ppermute(value, "lat", pairs + [(b, a) for a, b in pairs])

    x = fields.reshape(n, ch)
    edge = lax.dynamic_slice_in_dim(x, core * (n - EDGE), EDGE, axis=0)
    edge_y = swap(edge, 2)
    x_c = swap(x, 1)
    x_y = swap(x, 2)
    edge_d = swap(edge_y, 1)
    x_d = swap(x_y, 1)
    bias_own = jnp.pad(key_bias.reshape(n, H).T, ((0, 0), (0, width - n)))
    x_v, conv_w = load(x, conv_weight)
    near_parts = conv_half(me, x_v, x_c, edge_y, edge_d, conv_w)
    za = lat_swap(near_parts[0], 0)
    zb = lat_swap(near_parts[1], 1)
    near = residual_of(me, za, zb, near_parts[2], x_v, x_c, bias_own)
    far_y = swap(near, 2)
    near_c = swap(near, 1)
    far_d = swap(far_y, 1)
    far_parts = conv_half(me, x_y, x_d, x_v, x_c, conv_w)
    za = lat_swap(far_parts[0], 0)
    zb = lat_swap(far_parts[1], 1)
    far = residual_of(me, za, zb, far_parts[2], x_y, x_d)
    near_y = swap(far, 2)
    far_c = swap(far, 1)
    near_d = swap(near_y, 1)

    gain = norm_gain.reshape(lon_size, 1, width)
    k_far, v_far = keys_of(me, (far, far_c, far_y, far_d), gain, qkv_weight)
    out = attend(me, (near, near_c, near_y, near_d), gain, qkv_weight, k_far, v_far, far_y, far_d, out_weight)
    return out.reshape(fields.shape)


def solution(mesh):
    def on_device(*args):
        fields, conv_weight = args[0], args[1]
        special = (
            mesh.shape["lon"] == 4
            and fields.shape[0] == 1
            and conv_weight.shape[1] % 256 == 0
            and fields.shape[1] % 32 == 0
            and fields.shape[1] <= conv_weight.shape[1]
        )
        if not special:
            return general_device(*args)
        return four_shard_device(*args)

    return jax.shard_map(
        on_device,
        mesh=mesh,
        in_specs=(
            P(("ens", "lat"), "lon", None),
            P(None, "lon"),
            P(),
            P(),
            P(),
            P("lat", "lon", None),
        ),
        out_specs=P(("ens", "lat"), "lon", None),
        check_vma=False,
    )
```

```python
import functools
import math

import jax
import jax.numpy as jnp
from jax import lax
from jax.experimental import pallas as pl
from jax.experimental.pallas import tpu as pltpu
from jax.sharding import PartitionSpec as P


H = 16
EDGE = 16
PIECES = 8
F32 = jnp.float32
BF16 = jnp.bfloat16


def extended(block, sides, width):
    for axis, dim in sides:
        count = lax.axis_size(axis)
        forward = [(i, i + 1) for i in range(count - 1)]
        backward = [(target, source) for source, target in forward]
        low = lax.ppermute(
            lax.slice_in_dim(block, block.shape[dim] - width, None, axis=dim), axis, forward
        )
        high = lax.ppermute(lax.slice_in_dim(block, 0, width, axis=dim), axis, backward)
        block = jnp.concatenate([low, block, high], axis=dim)
    return block


def tap_sum(wrapped, conv_weight, out_rows, lon_total, channels):
    out_width = conv_weight.shape[1]
    accum_cols = jnp.zeros((out_rows * lon_total, out_width), jnp.float32)
    tap_idx = 0
    for step_lat in (-1, 0, 1):
        for step_lon in (-1, 0, 1):
            shifted = wrapped[
                1 + step_lat : 1 + step_lat + out_rows, 1 + step_lon : 1 + step_lon + lon_total
            ].reshape(out_rows * lon_total, channels)
            accum_cols = accum_cols + jnp.dot(
                shifted,
                conv_weight[tap_idx * channels : (tap_idx + 1) * channels],
                preferred_element_type=jnp.float32,
            )
            tap_idx += 1
    return accum_cols.reshape(out_rows, lon_total, out_width)


def general_device(fields, conv_weight, norm_gain, qkv_weight, out_weight, key_bias):
    lat_n, lon_n, channels = fields.shape
    row_count = lat_n * lon_n
    head_dim = channels // H
    score_scale = 1.0 / math.sqrt(head_dim)
    banded = extended(fields, (("lat", 0),), 1)
    circle = lax.all_gather(banded, "lon", axis=1, tiled=True)
    lon_total = circle.shape[1]
    wrapped = jnp.concatenate([circle[:, -1:], circle, circle[:, :1]], axis=1)
    out_cols = tap_sum(wrapped, conv_weight, lat_n, lon_total, channels).astype(jnp.bfloat16)
    conv_out = lax.all_to_all(out_cols, "lon", split_axis=1, concat_axis=2, tiled=True).reshape(
        row_count, channels
    )
    residual = (
        fields.reshape(row_count, channels).astype(jnp.float32) + conv_out.astype(jnp.float32)
    ).astype(jnp.bfloat16)
    stream = residual.astype(jnp.float32)
    normed = (
        stream * lax.rsqrt(jnp.mean(stream * stream, axis=-1, keepdims=True) + 1e-06) * norm_gain
    ).astype(jnp.bfloat16)
    projected = jnp.dot(normed, qkv_weight, preferred_element_type=jnp.float32).astype(jnp.bfloat16)
    queries = projected[:, :channels].reshape(lat_n, lon_n, channels)
    key_rows = projected[:, channels : 2 * channels].reshape(lat_n, lon_n, channels)
    value_rows = projected[:, 2 * channels :].reshape(lat_n, lon_n, channels)
    query_heads = queries.reshape(lat_n, lon_n, H, head_dim)
    key_part = lax.all_gather(key_rows, "lon", axis=1, tiled=True)
    value_part = lax.all_gather(value_rows, "lon", axis=1, tiled=True)
    bias_part = lax.all_gather(key_bias, "lon", axis=1, tiled=True)
    span = key_part.shape[1]
    key_heads = key_part.reshape(lat_n, span, H, head_dim)
    value_heads = value_part.reshape(lat_n, span, H, head_dim)
    scores = (
        jnp.einsum("aqhd,akhd->ahqk", query_heads, key_heads, preferred_element_type=jnp.float32)
        * score_scale
    )
    scores = scores + jnp.transpose(bias_part, (0, 2, 1)).astype(jnp.float32)[:, :, None, :]
    weights = jnp.exp(scores - jnp.max(scores, axis=-1)[..., None])
    denom = jnp.sum(weights, axis=-1)
    accum = jnp.einsum(
        "ahqk,akhd->ahqd",
        weights.astype(jnp.bfloat16),
        value_heads,
        preferred_element_type=jnp.float32,
    )
    attended = (
        jnp.transpose(accum / denom[..., None], (0, 2, 1, 3))
        .reshape(row_count, channels)
        .astype(jnp.bfloat16)
    )
    mixed = residual.astype(jnp.float32) + jnp.dot(
        attended, out_weight, preferred_element_type=jnp.float32
    )
    return mixed.astype(jnp.bfloat16).reshape(lat_n, lon_n, channels)


VMEM = pltpu.VMEM
ANY = pl.ANY


def vspec():
    return pl.BlockSpec(memory_space=VMEM)


def sspec():
    return pl.BlockSpec(memory_space=pltpu.SMEM)


def aspec():
    return pl.BlockSpec(memory_space=ANY)


def vout(shape, dtype):
    return VMEM(shape, dtype)


def load_kernel(*refs):
    count = (len(refs) - 1) // 2
    sem = refs[-1]
    copies = []
    for src, dst in zip(refs[:count], refs[count : 2 * count]):
        rows = src.shape[0]
        pieces = PIECES if rows % (16 * PIECES) == 0 else 1
        size = rows // pieces
        for p in range(pieces):
            at = pl.ds(p * size, size)
            copy = pltpu.make_async_copy(src.at[at], dst.at[at], sem.at[len(copies)])
            copy.start()
            copies.append(copy)
    for copy in copies:
        copy.wait()


def load(*arrays):
    total = sum(a.size * a.dtype.itemsize for a in arrays)
    return pl.pallas_call(
        load_kernel,
        out_shape=tuple(vout(a.shape, a.dtype) for a in arrays),
        in_specs=[aspec()] * len(arrays),
        out_specs=tuple(vspec() for _ in arrays),
        scratch_shapes=[pltpu.SemaphoreType.DMA((PIECES * len(arrays),))],
        compiler_params=pltpu.CompilerParams(vmem_limit_bytes=1 << 20),
        cost_estimate=pl.CostEstimate(flops=0, bytes_accessed=total, transcendentals=0),
        name="load",
    )(*[pltpu.with_memory_space_constraint(a, pltpu.HBM) for a in arrays])


def conv_kernel(me, xa, xb, ea, eb, w, first, second, mid, ext, cols):
    n, ch = xa.shape
    core = me[0] % 2
    if ea.shape[0] == EDGE:
        edge_a, edge_b = ea[...], eb[...]
    else:
        edge_a = ea[pl.ds(pl.multiple_of(core * (n - EDGE), 16), EDGE), :]
        edge_b = eb[pl.ds(pl.multiple_of((1 - core) * (n - EDGE), 16), EDGE), :]
    odd = me[1] % 2
    ext[pl.ds(pl.multiple_of(EDGE + core * n, 16), n), :] = xa[...]
    ext[pl.ds(pl.multiple_of(EDGE + (1 - core) * n, 16), n), :] = xb[...]
    far = EDGE + 2 * n
    ext[pl.ds(pl.multiple_of((1 - core) * far, 16), EDGE), :] = edge_a
    ext[pl.ds(pl.multiple_of(core * far, 16), EDGE), :] = edge_b
    for b in range(3):
        cols[:, b * ch : (b + 1) * ch] = ext[EDGE - 1 + b : EDGE - 1 + b + 2 * n, :]
    for a, out in ((2 * odd, first), (2 - 2 * odd, second), (1, mid)):
        taps = w[pl.ds(pl.multiple_of(a * 3 * ch, 16), 3 * ch), :]
        out[...] = jnp.dot(cols[...], taps, preferred_element_type=F32).astype(out.dtype)


def conv_half(me, xa, xb, ea, eb, w):
    n, ch = xa.shape
    width = w.shape[1]
    return pl.pallas_call(
        conv_kernel,
        out_shape=(
            vout((2 * n, width), BF16),
            vout((2 * n, width), BF16),
            vout((2 * n, width), F32),
        ),
        in_specs=[sspec()] + [vspec()] * 5,
        out_specs=(vspec(),) * 3,
        scratch_shapes=[
            VMEM((2 * n + 2 * EDGE, ch), BF16),
            VMEM((2 * n, 3 * ch), BF16),
        ],
        compiler_params=pltpu.CompilerParams(vmem_limit_bytes=12 << 20),
        cost_estimate=pl.CostEstimate(
            flops=2 * 2 * n * 9 * ch * width, bytes_accessed=2 * 9 * ch * width, transcendentals=0
        ),
        name="conv_half",
    )(me, xa, xb, ea, eb, w)


def residual_kernel(me, first, second, mid, xa, xb, *rest):
    out = rest[-1]
    n = xa.shape[0]
    width = mid.shape[1]
    lane = me[0]
    core = lane % 2
    inner = jnp.logical_and(me[1] > 0, me[1] < me[2] - 1)
    at = pl.ds(pl.multiple_of(lane * width, width), width)
    for x, place in ((xa, core), (xb, 1 - core)):
        rows = pl.ds(pl.multiple_of(place * n, 16), n)
        south = second[rows, :].astype(F32)
        south = jnp.where(inner, south, jnp.zeros_like(south))
        conv_out = first[rows, :].astype(F32) + south + mid[rows, :]
        out[rows, :] = (x[:, at].astype(F32) + conv_out.astype(BF16).astype(F32)).astype(BF16)
    if len(rest) == 2:
        out[2 * n : 2 * n + H, :] = rest[0][...]


def residual_of(me, first, second, mid, xa, xb, *extra):
    rows, width = mid.shape
    rows += H * len(extra)
    return pl.pallas_call(
        residual_kernel,
        out_shape=vout((rows, width), BF16),
        in_specs=[sspec()] + [vspec()] * (5 + len(extra)),
        out_specs=vspec(),
        compiler_params=pltpu.CompilerParams(vmem_limit_bytes=4 << 20),
        cost_estimate=pl.CostEstimate(
            flops=4 * rows * width, bytes_accessed=8 * rows * width, transcendentals=0
        ),
        name="residual_of",
    )(me, first, second, mid, xa, xb, *extra)


def normed_of(blocks, gain, lane, ch, rows):
    streams = [b[0:rows, :].astype(F32) for b in blocks]
    square = sum(jnp.sum(s * s, axis=-1, keepdims=True) for s in streams)
    factor = lax.rsqrt(square * (1.0 / ch) + 1e-06)
    return [(s * factor * gain[lane ^ k]).astype(BF16) for k, s in enumerate(streams)]


def keys_kernel(me, b0, b1, b2, b3, gain, w, k_out, v_out):
    lane = me[0]
    rows, ch = k_out.shape
    width = b0.shape[1]
    parts = normed_of((b0, b1, b2, b3), gain, lane, ch, rows)
    for out, first in ((k_out, ch), (v_out, 2 * ch)):
        acc = None
        for k, part in enumerate(parts):
            at = pl.multiple_of((lane ^ k) * width, width)
            term = jnp.dot(part, w[pl.ds(at, width), first : first + ch], preferred_element_type=F32)
            acc = term if acc is None else acc + term
        out[...] = acc.astype(BF16)


def keys_of(me, blocks, gain, w):
    rows = blocks[0].shape[0]
    ch = w.shape[0]
    out = vout((rows, ch), BF16)
    return pl.pallas_call(
        keys_kernel,
        out_shape=(out, out),
        in_specs=[sspec()] + [vspec()] * 6,
        out_specs=(vspec(), vspec()),
        compiler_params=pltpu.CompilerParams(vmem_limit_bytes=24 << 20),
        cost_estimate=pl.CostEstimate(
            flops=2 * rows * ch * 2 * ch, bytes_accessed=4 * ch * ch, transcendentals=0
        ),
        name="keys_of",
    )(me, *blocks, gain, w)


def scaled(block, gain, lane, k, rows):
    return (block[0:rows, :].astype(F32) * gain[lane ^ k]).astype(BF16)


def project_kernel(steps, me, gain, w, *refs):
    lane = me[0]
    blocks = refs[: len(steps)]
    olds = refs[len(steps) : -3]
    keys, values, query = refs[-3:]
    rows, ch = keys.shape
    n = query.shape[0]
    width = blocks[0].shape[1]
    own = pl.multiple_of((lane % 2) * n, 16)
    parts = [scaled(b, gain, lane, k, rows) for b, k in zip(blocks, steps)]
    owns = [
        (b[pl.ds(own, n), :].astype(F32) * gain[lane ^ k]).astype(BF16)
        for b, k in zip(blocks, steps)
    ]
    for i, (first, out, use) in enumerate(
        ((ch, keys, parts), (2 * ch, values, parts), (0, query, owns))
    ):
        acc = olds[i][...] if olds else None
        for k, part in zip(steps, use):
            at = pl.multiple_of((lane ^ k) * width, width)
            term = jnp.dot(part, w[pl.ds(at, width), first : first + ch], preferred_element_type=F32)
            acc = term if acc is None else acc + term
        out[...] = acc


def project(me, steps, blocks, gain, w, n, olds=()):
    rows = 2 * n
    ch, width = w.shape[0], blocks[0].shape[1]
    return pl.pallas_call(
        functools.partial(project_kernel, steps),
        out_shape=(vout((rows, ch), F32), vout((rows, ch), F32), vout((n, ch), F32)),
        in_specs=[sspec()] + [vspec()] * (2 + len(blocks) + len(olds)),
        out_specs=(vspec(),) * 3,
        input_output_aliases={3 + len(blocks) + i: i for i in range(len(olds))},
        compiler_params=pltpu.CompilerParams(vmem_limit_bytes=16 << 20),
        cost_estimate=pl.CostEstimate(
            flops=2 * (2 * rows + n) * width * len(blocks) * ch,
            bytes_accessed=6 * ch * width * len(blocks),
            transcendentals=0,
        ),
        name="project",
    )(me, gain, w, *blocks, *olds)


def attend_kernel(
    steps, me, b0, b1, b2, b3, gain, w, key_sum, value_sum, query_sum, k_far, v_far, bias_y, bias_d,
    w_out, out, keys, values, query, attended
):
    lane = me[0]
    core = lane % 2
    n, ch = out.shape
    rows = 2 * n
    width = b0.shape[1]
    hd = ch // H
    blocks = (b0, b1, b2, b3)
    own = pl.multiple_of(core * n, 16)

    def factor_of(at, count):
        square = 0.0
        for b in blocks:
            stream = b[pl.ds(at, count), :].astype(F32)
            square = square + jnp.sum(stream * stream, axis=-1, keepdims=True)
        return lax.rsqrt(square * (1.0 / ch) + 1e-06)

    for first, dst, acc, at, count in (
        (0, query, query_sum, own, n),
        (ch, keys, key_sum, 0, rows),
        (2 * ch, values, value_sum, 0, rows),
    ):
        total = acc[...]
        for k in steps:
            part = (blocks[k][pl.ds(at, count), :].astype(F32) * gain[lane ^ k]).astype(BF16)
            place = pl.multiple_of((lane ^ k) * width, width)
            total = total + jnp.dot(
                part, w[pl.ds(place, width), first : first + ch], preferred_element_type=F32
            )
        dst[0:count, :] = (total * factor_of(at, count)).astype(BF16)
    keys[rows : 2 * rows, :] = k_far[...]
    values[rows : 2 * rows, :] = v_far[...]
    pieces = []
    for a, c in ((b0, b1), (bias_y, bias_d)):
        a, c = (v[rows : rows + H, 0:n].astype(F32) for v in (a, c))
        pieces += [jnp.where(core == 0, a, c), jnp.where(core == 0, c, a)]
    bias = jnp.concatenate(pieces, axis=1)
    group = 256 // hd
    head_of = lax.broadcasted_iota(jnp.int32, (n, 256), 1) // hd
    for g in range(ch // 256):
        cols = slice(g * 256, (g + 1) * 256)
        q = query[:, cols] * jnp.asarray(1.0 / math.sqrt(hd), BF16)
        stacked = jnp.concatenate(
            [jnp.where(head_of == t, q, jnp.zeros_like(q)) for t in range(group)], axis=0
        )
        scores = lax.dot_general(
            stacked, keys[:, cols], (((1,), (1,)), ((), ())), preferred_element_type=F32
        )
        values_g = values[:, cols]
        result = jnp.zeros((n, 256), F32)
        for t in range(group):
            head = g * group + t
            s = scores[t * n : (t + 1) * n] + bias[head : head + 1, :]
            e = jnp.exp(s - jnp.max(s, axis=-1, keepdims=True))
            total = jnp.sum(e, axis=-1, keepdims=True)
            o = jnp.dot(e.astype(BF16), values_g, preferred_element_type=F32)
            result = jnp.where(head_of == t, o / total, result)
        attended[:, cols] = result.astype(BF16)
    for k, block in enumerate(blocks):
        at = pl.multiple_of((lane ^ k) * width, width)
        mixed = block[pl.ds(own, n), :].astype(F32) + jnp.dot(
            attended[...], w_out[:, pl.ds(at, width)], preferred_element_type=F32
        )
        out[:, pl.ds(at, width)] = mixed.astype(BF16)


def attend(me, steps, blocks, gain, w, sums, k_far, v_far, bias_y, bias_d, w_out):
    rows, ch = k_far.shape
    n = rows // 2
    return pl.pallas_call(
        functools.partial(attend_kernel, steps),
        out_shape=jax.ShapeDtypeStruct((n, ch), BF16),
        in_specs=[sspec()] + [vspec()] * 14,
        out_specs=vspec(),
        scratch_shapes=[
            VMEM((2 * rows, ch), BF16),
            VMEM((2 * rows, ch), BF16),
            VMEM((n, ch), BF16),
            VMEM((n, ch), BF16),
        ],
        compiler_params=pltpu.CompilerParams(vmem_limit_bytes=32 << 20),
        cost_estimate=pl.CostEstimate(
            flops=2 * rows * ch * ch + 4 * n * 2 * rows * ch * 4,
            bytes_accessed=8 * ch * ch,
            transcendentals=n * 2 * rows * H,
        ),
        name="attend",
    )(me, *blocks, gain, w, *sums, k_far, v_far, bias_y, bias_d, w_out)


def four_shard_device(fields, conv_weight, norm_gain, qkv_weight, out_weight, key_bias):
    _, n, ch = fields.shape
    width = conv_weight.shape[1]
    lane = lax.axis_index("lon")
    core = lane % 2
    me = jnp.stack([lane, lax.axis_index("lat"), lax.axis_size("lat")]).astype(jnp.int32)
    lon_size = lax.axis_size("lon")
    lat_size = lax.axis_size("lat")

    def swap(value, bit):
        return lax.ppermute(value, "lon", [(i, i ^ bit) for i in range(lon_size)])

    def lat_swap(value, first):
        def target(i):
            j = i + 1 if (i - first) % 2 == 0 else i - 1
            return j if 0 <= j < lat_size else i

        pairs = []
        for m in range(lon_size):
            for i in range(lat_size):
                j = target(i)
                to = (m, j) if j != i else (m ^ 1, i)
                pairs.append((m * lat_size + i, to[0] * lat_size + to[1]))
        return lax.ppermute(value, ("lon", "lat"), pairs)

    x = fields.reshape(n, ch)
    edge = lax.dynamic_slice_in_dim(x, core * (n - EDGE), EDGE, axis=0)
    edge_y = swap(edge, 2)
    x_c = swap(x, 1)
    x_y = swap(x, 2)
    edge_d = swap(edge_y, 1)
    x_d = swap(x_y, 1)
    bias_own = jnp.pad(key_bias.reshape(n, H).T, ((0, 0), (0, width - n)))
    x_v, conv_w = load(x, conv_weight)
    near_parts = conv_half(me, x_v, x_c, edge_y, edge_d, conv_w)
    za = lat_swap(near_parts[0], 0)
    zb = lat_swap(near_parts[1], 1)
    near = residual_of(me, za, zb, near_parts[2], x_v, x_c, bias_own)
    far_y = swap(near, 2)
    near_c = swap(near, 1)
    far_d = swap(far_y, 1)
    far_parts = conv_half(me, x_y, x_d, x_v, x_c, conv_w)
    za = lat_swap(far_parts[0], 0)
    zb = lat_swap(far_parts[1], 1)
    far = residual_of(me, za, zb, far_parts[2], x_y, x_d)
    near_y = swap(far, 2)
    far_c = swap(far, 1)
    near_d = swap(near_y, 1)

    gain = norm_gain.reshape(lon_size, 1, width)
    k_far, v_far = keys_of(me, (far, far_c, far_y, far_d), gain, qkv_weight)
    sums = project(me, (0, 1), (near, near_c), gain, qkv_weight, n)
    sums = project(me, (2,), (near_y,), gain, qkv_weight, n, sums)
    out = attend(
        me, (3,), (near, near_c, near_y, near_d), gain, qkv_weight, sums, k_far, v_far, far_y,
        far_d, out_weight
    )
    return out.reshape(fields.shape)


def solution(mesh):
    def on_device(*args):
        fields, conv_weight = args[0], args[1]
        special = (
            mesh.shape["lon"] == 4
            and fields.shape[0] == 1
            and conv_weight.shape[1] % 256 == 0
            and fields.shape[1] % 32 == 0
            and fields.shape[1] <= conv_weight.shape[1]
        )
        if not special:
            return general_device(*args)
        return four_shard_device(*args)

    return jax.shard_map(
        on_device,
        mesh=mesh,
        in_specs=(
            P(("ens", "lat"), "lon", None),
            P(None, "lon"),
            P(),
            P(),
            P(),
            P("lat", "lon", None),
        ),
        out_specs=P(("ens", "lat"), "lon", None),
        check_vma=False,
    )
```

```python
import functools
import math

import jax
import jax.numpy as jnp
from jax import lax
from jax.experimental import pallas as pl
from jax.experimental.pallas import tpu as pltpu
from jax.sharding import PartitionSpec as P


H = 16
EDGE = 16
PIECES = 8
F32 = jnp.float32
BF16 = jnp.bfloat16


def extended(block, sides, width):
    for axis, dim in sides:
        count = lax.axis_size(axis)
        forward = [(i, i + 1) for i in range(count - 1)]
        backward = [(target, source) for source, target in forward]
        low = lax.ppermute(
            lax.slice_in_dim(block, block.shape[dim] - width, None, axis=dim), axis, forward
        )
        high = lax.ppermute(lax.slice_in_dim(block, 0, width, axis=dim), axis, backward)
        block = jnp.concatenate([low, block, high], axis=dim)
    return block


def tap_sum(wrapped, conv_weight, out_rows, lon_total, channels):
    out_width = conv_weight.shape[1]
    accum_cols = jnp.zeros((out_rows * lon_total, out_width), jnp.float32)
    tap_idx = 0
    for step_lat in (-1, 0, 1):
        for step_lon in (-1, 0, 1):
            shifted = wrapped[
                1 + step_lat : 1 + step_lat + out_rows, 1 + step_lon : 1 + step_lon + lon_total
            ].reshape(out_rows * lon_total, channels)
            accum_cols = accum_cols + jnp.dot(
                shifted,
                conv_weight[tap_idx * channels : (tap_idx + 1) * channels],
                preferred_element_type=jnp.float32,
            )
            tap_idx += 1
    return accum_cols.reshape(out_rows, lon_total, out_width)


def general_device(fields, conv_weight, norm_gain, qkv_weight, out_weight, key_bias):
    lat_n, lon_n, channels = fields.shape
    row_count = lat_n * lon_n
    head_dim = channels // H
    score_scale = 1.0 / math.sqrt(head_dim)
    banded = extended(fields, (("lat", 0),), 1)
    circle = lax.all_gather(banded, "lon", axis=1, tiled=True)
    lon_total = circle.shape[1]
    wrapped = jnp.concatenate([circle[:, -1:], circle, circle[:, :1]], axis=1)
    out_cols = tap_sum(wrapped, conv_weight, lat_n, lon_total, channels).astype(jnp.bfloat16)
    conv_out = lax.all_to_all(out_cols, "lon", split_axis=1, concat_axis=2, tiled=True).reshape(
        row_count, channels
    )
    residual = (
        fields.reshape(row_count, channels).astype(jnp.float32) + conv_out.astype(jnp.float32)
    ).astype(jnp.bfloat16)
    stream = residual.astype(jnp.float32)
    normed = (
        stream * lax.rsqrt(jnp.mean(stream * stream, axis=-1, keepdims=True) + 1e-06) * norm_gain
    ).astype(jnp.bfloat16)
    projected = jnp.dot(normed, qkv_weight, preferred_element_type=jnp.float32).astype(jnp.bfloat16)
    queries = projected[:, :channels].reshape(lat_n, lon_n, channels)
    key_rows = projected[:, channels : 2 * channels].reshape(lat_n, lon_n, channels)
    value_rows = projected[:, 2 * channels :].reshape(lat_n, lon_n, channels)
    query_heads = queries.reshape(lat_n, lon_n, H, head_dim)
    key_part = lax.all_gather(key_rows, "lon", axis=1, tiled=True)
    value_part = lax.all_gather(value_rows, "lon", axis=1, tiled=True)
    bias_part = lax.all_gather(key_bias, "lon", axis=1, tiled=True)
    span = key_part.shape[1]
    key_heads = key_part.reshape(lat_n, span, H, head_dim)
    value_heads = value_part.reshape(lat_n, span, H, head_dim)
    scores = (
        jnp.einsum("aqhd,akhd->ahqk", query_heads, key_heads, preferred_element_type=jnp.float32)
        * score_scale
    )
    scores = scores + jnp.transpose(bias_part, (0, 2, 1)).astype(jnp.float32)[:, :, None, :]
    weights = jnp.exp(scores - jnp.max(scores, axis=-1)[..., None])
    denom = jnp.sum(weights, axis=-1)
    accum = jnp.einsum(
        "ahqk,akhd->ahqd",
        weights.astype(jnp.bfloat16),
        value_heads,
        preferred_element_type=jnp.float32,
    )
    attended = (
        jnp.transpose(accum / denom[..., None], (0, 2, 1, 3))
        .reshape(row_count, channels)
        .astype(jnp.bfloat16)
    )
    mixed = residual.astype(jnp.float32) + jnp.dot(
        attended, out_weight, preferred_element_type=jnp.float32
    )
    return mixed.astype(jnp.bfloat16).reshape(lat_n, lon_n, channels)


VMEM = pltpu.VMEM
ANY = pl.ANY


def vspec():
    return pl.BlockSpec(memory_space=VMEM)


def sspec():
    return pl.BlockSpec(memory_space=pltpu.SMEM)


def aspec():
    return pl.BlockSpec(memory_space=ANY)


def vout(shape, dtype):
    return VMEM(shape, dtype)


def load_kernel(pieces, *refs):
    count = (len(refs) - 1) // 2
    sem = refs[-1]
    copies = []
    for src, dst, parts in zip(refs[:count], refs[count : 2 * count], pieces):
        place = 0
        for start, size in parts:
            copy = pltpu.make_async_copy(
                src.at[pl.ds(start, size)], dst.at[pl.ds(place, size)], sem.at[len(copies)]
            )
            copy.start()
            copies.append(copy)
            place += size
    for copy in copies:
        copy.wait()


def load(arrays, ranges):
    pieces, shapes = [], []
    for a, spans in zip(arrays, ranges):
        parts = []
        for start, size in spans:
            cut = size // PIECES if size % (16 * PIECES) == 0 else size
            parts += [(start + at, cut) for at in range(0, size, cut)]
        pieces.append(tuple(parts))
        shapes.append(vout((sum(size for _, size in spans),) + a.shape[1:], a.dtype))
    total = sum(math.prod(v.shape) * 2 for v in shapes)
    return pl.pallas_call(
        functools.partial(load_kernel, tuple(pieces)),
        out_shape=tuple(shapes),
        in_specs=[aspec()] * len(arrays),
        out_specs=tuple(vspec() for _ in arrays),
        scratch_shapes=[pltpu.SemaphoreType.DMA((sum(len(p) for p in pieces),))],
        compiler_params=pltpu.CompilerParams(vmem_limit_bytes=1 << 20),
        cost_estimate=pl.CostEstimate(flops=0, bytes_accessed=total, transcendentals=0),
        name="load",
    )(*[pltpu.with_memory_space_constraint(a, pltpu.HBM) for a in arrays])


def conv_kernel(me, xa, xb, ea, eb, w, first, second, cols, ext):
    n, ch = xa.shape
    core = me[0] % 2
    odd = me[1] % 2
    if ea.shape[0] == EDGE:
        edge_a, edge_b = ea[...], eb[...]
    else:
        edge_a = ea[pl.ds(pl.multiple_of(core * (n - EDGE), 16), EDGE), :]
        edge_b = eb[pl.ds(pl.multiple_of((1 - core) * (n - EDGE), 16), EDGE), :]
    ext[pl.ds(pl.multiple_of(EDGE + core * n, 16), n), :] = xa[...]
    ext[pl.ds(pl.multiple_of(EDGE + (1 - core) * n, 16), n), :] = xb[...]
    far = EDGE + 2 * n
    ext[pl.ds(pl.multiple_of((1 - core) * far, 16), EDGE), :] = edge_a
    ext[pl.ds(pl.multiple_of(core * far, 16), EDGE), :] = edge_b
    for b in range(3):
        cols[:, b * ch : (b + 1) * ch] = ext[EDGE - 1 + b : EDGE - 1 + b + 2 * n, :]
    for a, out in ((odd, first), (1 - odd, second)):
        taps = w[pl.ds(pl.multiple_of(a * 3 * ch, 16), 3 * ch), :]
        out[...] = jnp.dot(cols[...], taps, preferred_element_type=F32).astype(out.dtype)


def conv_sides(me, xa, xb, ea, eb, w):
    n, ch = xa.shape
    width = w.shape[1]
    return pl.pallas_call(
        conv_kernel,
        out_shape=(
            vout((2 * n, width), BF16),
            vout((2 * n, width), BF16),
            vout((2 * n, 3 * ch), BF16),
        ),
        in_specs=[sspec()] + [vspec()] * 5,
        out_specs=(vspec(),) * 3,
        scratch_shapes=[VMEM((2 * n + 2 * EDGE, ch), BF16)],
        compiler_params=pltpu.CompilerParams(vmem_limit_bytes=6 << 20),
        cost_estimate=pl.CostEstimate(
            flops=2 * 2 * n * 6 * ch * width, bytes_accessed=2 * 6 * ch * width, transcendentals=0
        ),
        name="conv_sides",
    )(me, xa, xb, ea, eb, w)


def middle_kernel(me, cols, w, mid, own, valid):
    lane = me[0]
    ch = cols.shape[1] // 3
    width = mid.shape[1]
    mid[...] = jnp.dot(cols[...], w[...], preferred_element_type=F32)
    own[...] = cols[:, pl.ds(pl.multiple_of(ch + lane * width, width), width)].astype(F32)
    inner = jnp.logical_and(me[1] > 0, me[1] < me[2] - 1)
    valid[...] = jnp.where(inner, jnp.ones(valid.shape, F32), jnp.zeros(valid.shape, F32))


def conv_middle(me, cols, w):
    rows, depth = cols.shape
    width = w.shape[1]
    return pl.pallas_call(
        middle_kernel,
        out_shape=(
            vout((rows, width), F32),
            vout((rows, width), F32),
            vout((1, width), F32),
        ),
        in_specs=[sspec(), vspec(), vspec()],
        out_specs=(vspec(),) * 3,
        compiler_params=pltpu.CompilerParams(vmem_limit_bytes=4 << 20),
        cost_estimate=pl.CostEstimate(
            flops=2 * rows * depth * width, bytes_accessed=2 * depth * width, transcendentals=0
        ),
        name="conv_middle",
    )(me, cols, w)


def residual_of(first, second, mid, own, valid):
    south = jnp.where(valid > 0.5, second.astype(F32), 0.0)
    conv_out = (first.astype(F32) + south + mid).astype(BF16)
    return (own + conv_out.astype(F32)).astype(BF16)


def joined_kernel(first, second, mid, own, valid, bias, out):
    rows = mid.shape[0]
    out[0:rows, :] = residual_of(
        first[...], second[...], mid[...], own[...], valid[...]
    )
    out[rows : rows + H, :] = bias[...]


def joined_residual(first, second, mid, own, valid, bias):
    rows, width = mid.shape
    return pl.pallas_call(
        joined_kernel,
        out_shape=vout((rows + H, width), BF16),
        in_specs=[vspec()] * 6,
        out_specs=vspec(),
        compiler_params=pltpu.CompilerParams(vmem_limit_bytes=2 << 20),
        cost_estimate=pl.CostEstimate(
            flops=4 * rows * width, bytes_accessed=8 * rows * width, transcendentals=0
        ),
        name="joined_residual",
    )(first, second, mid, own, valid, bias)


def factor_of(blocks, at, count, ch):
    square = 0.0
    for b in blocks:
        stream = b[pl.ds(at, count), :].astype(F32)
        square = square + jnp.sum(stream * stream, axis=-1, keepdims=True)
    return lax.rsqrt(square * (1.0 / ch) + 1e-06)


def keys_kernel(steps, me, b0, b1, b2, b3, gain, w, key_sum, value_sum, k_out, v_out):
    lane = me[0]
    rows, ch = k_out.shape
    width = b0.shape[1]
    blocks = (b0, b1, b2, b3)
    parts = [scaled(blocks[k], gain, lane, k, rows) for k in steps]
    factor = factor_of(blocks, 0, rows, ch)
    for out, acc, first in ((k_out, key_sum, ch), (v_out, value_sum, 2 * ch)):
        total = acc[...]
        for k, part in zip(steps, parts):
            at = pl.multiple_of((lane ^ k) * width, width)
            total = total + jnp.dot(
                part, w[pl.ds(at, width), first : first + ch], preferred_element_type=F32
            )
        out[...] = (total * factor).astype(BF16)


def keys_of(me, steps, blocks, gain, w, sums):
    rows = blocks[0].shape[0]
    ch = w.shape[0]
    out = vout((rows, ch), BF16)
    return pl.pallas_call(
        functools.partial(keys_kernel, steps),
        out_shape=(out, out),
        in_specs=[sspec()] + [vspec()] * 8,
        out_specs=(vspec(), vspec()),
        compiler_params=pltpu.CompilerParams(vmem_limit_bytes=16 << 20),
        cost_estimate=pl.CostEstimate(
            flops=2 * rows * ch * ch, bytes_accessed=2 * ch * ch, transcendentals=0
        ),
        name="keys_of",
    )(me, *blocks, gain, w, *sums)


def scaled(block, gain, lane, k, rows):
    return (block[0:rows, :].astype(F32) * gain[lane ^ k]).astype(BF16)


def project_kernel(steps, count, me, gain, w, *refs):
    lane = me[0]
    blocks = refs[: len(steps)]
    olds = refs[len(steps) : -count]
    outs = refs[-count:]
    rows, ch = outs[0].shape
    n = rows // 2
    width = blocks[0].shape[1]
    own = pl.multiple_of((lane % 2) * n, 16)
    parts = [scaled(b, gain, lane, k, rows) for b, k in zip(blocks, steps)]
    owns = [
        (b[pl.ds(own, n), :].astype(F32) * gain[lane ^ k]).astype(BF16)
        for b, k in zip(blocks, steps)
    ]
    for i, out in enumerate(outs):
        first, use = ((ch, parts), (2 * ch, parts), (0, owns))[i]
        acc = olds[i][...] if olds else None
        for k, part in zip(steps, use):
            at = pl.multiple_of((lane ^ k) * width, width)
            term = jnp.dot(part, w[pl.ds(at, width), first : first + ch], preferred_element_type=F32)
            acc = term if acc is None else acc + term
        out[...] = acc


def project(me, steps, blocks, gain, w, n, olds=(), count=3):
    rows = 2 * n
    ch, width = w.shape[0], blocks[0].shape[1]
    return pl.pallas_call(
        functools.partial(project_kernel, steps, count),
        out_shape=(vout((rows, ch), F32), vout((rows, ch), F32), vout((n, ch), F32))[:count],
        in_specs=[sspec()] + [vspec()] * (2 + len(blocks) + len(olds)),
        out_specs=(vspec(),) * count,
        input_output_aliases={3 + len(blocks) + i: i for i in range(len(olds))},
        compiler_params=pltpu.CompilerParams(vmem_limit_bytes=16 << 20),
        cost_estimate=pl.CostEstimate(
            flops=2 * (2 * rows + n) * width * len(blocks) * ch,
            bytes_accessed=6 * ch * width * len(blocks),
            transcendentals=0,
        ),
        name="project",
    )(me, gain, w, *blocks, *olds)


def attend_kernel(
    steps, me, b0, b1, b2, b3, gain, w, key_sum, value_sum, query_sum, k_far, v_far, bias_y, bias_d,
    w_out, out, keys, values, query, attended
):
    lane = me[0]
    core = lane % 2
    n, ch = out.shape
    rows = 2 * n
    width = b0.shape[1]
    hd = ch // H
    blocks = (b0, b1, b2, b3)
    own = pl.multiple_of(core * n, 16)

    for first, dst, acc, at, count in (
        (0, query, query_sum, own, n),
        (ch, keys, key_sum, 0, rows),
        (2 * ch, values, value_sum, 0, rows),
    ):
        total = acc[...]
        for k in steps:
            part = (blocks[k][pl.ds(at, count), :].astype(F32) * gain[lane ^ k]).astype(BF16)
            place = pl.multiple_of((lane ^ k) * width, width)
            total = total + jnp.dot(
                part, w[pl.ds(place, width), first : first + ch], preferred_element_type=F32
            )
        dst[0:count, :] = (total * factor_of(blocks, at, count, ch)).astype(BF16)
    keys[rows : 2 * rows, :] = k_far[...]
    values[rows : 2 * rows, :] = v_far[...]
    pieces = []
    for a, c in ((b0, b1), (bias_y, bias_d)):
        a, c = (v[rows : rows + H, 0:n].astype(F32) for v in (a, c))
        pieces += [jnp.where(core == 0, a, c), jnp.where(core == 0, c, a)]
    bias = jnp.concatenate(pieces, axis=1)
    group = 256 // hd
    head_of = lax.broadcasted_iota(jnp.int32, (n, 256), 1) // hd
    for g in range(ch // 256):
        cols = slice(g * 256, (g + 1) * 256)
        q = query[:, cols] * jnp.asarray(1.0 / math.sqrt(hd), BF16)
        stacked = jnp.concatenate(
            [jnp.where(head_of == t, q, jnp.zeros_like(q)) for t in range(group)], axis=0
        )
        scores = lax.dot_general(
            stacked, keys[:, cols], (((1,), (1,)), ((), ())), preferred_element_type=F32
        )
        parts, totals = [], []
        for t in range(group):
            head = g * group + t
            s = scores[t * n : (t + 1) * n] + bias[head : head + 1, :]
            e = jnp.exp(s - jnp.max(s, axis=-1, keepdims=True))
            totals.append(jnp.sum(e, axis=-1, keepdims=True))
            parts.append(e.astype(BF16))
        summed = jnp.dot(
            jnp.concatenate(parts, axis=0), values[:, cols], preferred_element_type=F32
        )
        result = jnp.zeros((n, 256), F32)
        for t in range(group):
            result = jnp.where(head_of == t, summed[t * n : (t + 1) * n] / totals[t], result)
        attended[:, cols] = result.astype(BF16)
    for k, block in enumerate(blocks):
        at = pl.multiple_of((lane ^ k) * width, width)
        mixed = block[pl.ds(own, n), :].astype(F32) + jnp.dot(
            attended[...], w_out[:, pl.ds(at, width)], preferred_element_type=F32
        )
        out[:, pl.ds(at, width)] = mixed.astype(BF16)


def attend(me, steps, blocks, gain, w, sums, k_far, v_far, bias_y, bias_d, w_out):
    rows, ch = k_far.shape
    n = rows // 2
    return pl.pallas_call(
        functools.partial(attend_kernel, steps),
        out_shape=jax.ShapeDtypeStruct((n, ch), BF16),
        in_specs=[sspec()] + [vspec()] * 14,
        out_specs=vspec(),
        scratch_shapes=[
            VMEM((2 * rows, ch), BF16),
            VMEM((2 * rows, ch), BF16),
            VMEM((n, ch), BF16),
            VMEM((n, ch), BF16),
        ],
        compiler_params=pltpu.CompilerParams(vmem_limit_bytes=32 << 20),
        cost_estimate=pl.CostEstimate(
            flops=2 * rows * ch * ch + 4 * n * 2 * rows * ch * 4,
            bytes_accessed=8 * ch * ch,
            transcendentals=n * 2 * rows * H,
        ),
        name="attend",
    )(me, *blocks, gain, w, *sums, k_far, v_far, bias_y, bias_d, w_out)


def four_shard_device(fields, conv_weight, norm_gain, qkv_weight, out_weight, key_bias):
    _, n, ch = fields.shape
    width = conv_weight.shape[1]
    lane = lax.axis_index("lon")
    core = lane % 2
    me = jnp.stack([lane, lax.axis_index("lat"), lax.axis_size("lat")]).astype(jnp.int32)
    lon_size = lax.axis_size("lon")
    lat_size = lax.axis_size("lat")

    def swap(value, bit):
        return lax.ppermute(value, "lon", [(i, i ^ bit) for i in range(lon_size)])

    def lat_swap(value, first):
        def target(i):
            j = i + 1 if (i - first) % 2 == 0 else i - 1
            return j if 0 <= j < lat_size else i

        pairs = []
        for m in range(lon_size):
            for i in range(lat_size):
                j = target(i)
                to = (m, j) if j != i else (m ^ 1, i)
                pairs.append((m * lat_size + i, to[0] * lat_size + to[1]))
        return lax.ppermute(value, ("lon", "lat"), pairs)

    x = fields.reshape(n, ch)
    edge = lax.dynamic_slice_in_dim(x, core * (n - EDGE), EDGE, axis=0)
    edge_y = swap(edge, 2)
    x_c = swap(x, 1)
    x_y = swap(x, 2)
    edge_d = swap(edge_y, 1)
    x_d = swap(x_y, 1)
    bias_own = jnp.pad(key_bias.reshape(n, H).T, ((0, 0), (0, width - n)))
    taps = 3 * ch
    x_v, side_w = load((x, conv_weight), (((0, n),), ((0, taps), (2 * taps, taps))))
    za, zb, cols = conv_sides(me, x_v, x_c, edge_y, edge_d, side_w)
    za = lat_swap(za, 0)
    zb = lat_swap(zb, 1)
    (mid_w,) = load((conv_weight,), (((taps, taps),),))
    mid, own, valid = conv_middle(me, cols, mid_w)
    near = joined_residual(za, zb, mid, own, valid, bias_own)
    near_c = swap(near, 1)
    far_y = swap(near, 2)
    far_d = swap(far_y, 1)
    za, zb, cols = conv_sides(me, x_y, x_d, x_v, x_c, side_w)
    za = lat_swap(za, 0)
    zb = lat_swap(zb, 1)
    mid, own, valid = conv_middle(me, cols, mid_w)
    far = residual_of(za, zb, mid, own, valid)
    near_y = swap(far, 2)
    far_c = swap(far, 1)
    near_d = swap(near_y, 1)

    gain = norm_gain.reshape(lon_size, 1, width)
    far_sums = project(me, (0, 1), (far, far_c), gain, qkv_weight, n, count=2)
    k_far, v_far = keys_of(
        me, (2, 3), (far, far_c, far_y, far_d), gain, qkv_weight, far_sums
    )
    sums = project(me, (0, 1), (near, near_c), gain, qkv_weight, n)
    sums = project(me, (2,), (near_y,), gain, qkv_weight, n, sums)
    out = attend(
        me, (3,), (near, near_c, near_y, near_d), gain, qkv_weight, sums, k_far, v_far, far_y,
        far_d, out_weight
    )
    return out.reshape(fields.shape)


def solution(mesh):
    def on_device(*args):
        fields, conv_weight = args[0], args[1]
        special = (
            mesh.shape["lon"] == 4
            and fields.shape[0] == 1
            and conv_weight.shape[1] % 256 == 0
            and fields.shape[1] % 32 == 0
            and fields.shape[1] <= conv_weight.shape[1]
        )
        if not special:
            return general_device(*args)
        return four_shard_device(*args)

    return jax.shard_map(
        on_device,
        mesh=mesh,
        in_specs=(
            P(("ens", "lat"), "lon", None),
            P(None, "lon"),
            P(),
            P(),
            P(),
            P("lat", "lon", None),
        ),
        out_specs=P(("ens", "lat"), "lon", None),
        check_vma=False,
    )
```

```python
import functools
import math

import jax
import jax.numpy as jnp
from jax import lax
from jax.experimental import pallas as pl
from jax.experimental.pallas import tpu as pltpu
from jax.sharding import PartitionSpec as P


H = 16
EDGE = 16
PIECES = 8
F32 = jnp.float32
BF16 = jnp.bfloat16


def extended(block, sides, width):
    for axis, dim in sides:
        count = lax.axis_size(axis)
        forward = [(i, i + 1) for i in range(count - 1)]
        backward = [(target, source) for source, target in forward]
        low = lax.ppermute(
            lax.slice_in_dim(block, block.shape[dim] - width, None, axis=dim), axis, forward
        )
        high = lax.ppermute(lax.slice_in_dim(block, 0, width, axis=dim), axis, backward)
        block = jnp.concatenate([low, block, high], axis=dim)
    return block


def tap_sum(wrapped, conv_weight, out_rows, lon_total, channels):
    out_width = conv_weight.shape[1]
    accum_cols = jnp.zeros((out_rows * lon_total, out_width), jnp.float32)
    tap_idx = 0
    for step_lat in (-1, 0, 1):
        for step_lon in (-1, 0, 1):
            shifted = wrapped[
                1 + step_lat : 1 + step_lat + out_rows, 1 + step_lon : 1 + step_lon + lon_total
            ].reshape(out_rows * lon_total, channels)
            accum_cols = accum_cols + jnp.dot(
                shifted,
                conv_weight[tap_idx * channels : (tap_idx + 1) * channels],
                preferred_element_type=jnp.float32,
            )
            tap_idx += 1
    return accum_cols.reshape(out_rows, lon_total, out_width)


def general_device(fields, conv_weight, norm_gain, qkv_weight, out_weight, key_bias):
    lat_n, lon_n, channels = fields.shape
    row_count = lat_n * lon_n
    head_dim = channels // H
    score_scale = 1.0 / math.sqrt(head_dim)
    banded = extended(fields, (("lat", 0),), 1)
    circle = lax.all_gather(banded, "lon", axis=1, tiled=True)
    lon_total = circle.shape[1]
    wrapped = jnp.concatenate([circle[:, -1:], circle, circle[:, :1]], axis=1)
    out_cols = tap_sum(wrapped, conv_weight, lat_n, lon_total, channels).astype(jnp.bfloat16)
    conv_out = lax.all_to_all(out_cols, "lon", split_axis=1, concat_axis=2, tiled=True).reshape(
        row_count, channels
    )
    residual = (
        fields.reshape(row_count, channels).astype(jnp.float32) + conv_out.astype(jnp.float32)
    ).astype(jnp.bfloat16)
    stream = residual.astype(jnp.float32)
    normed = (
        stream * lax.rsqrt(jnp.mean(stream * stream, axis=-1, keepdims=True) + 1e-06) * norm_gain
    ).astype(jnp.bfloat16)
    projected = jnp.dot(normed, qkv_weight, preferred_element_type=jnp.float32).astype(jnp.bfloat16)
    queries = projected[:, :channels].reshape(lat_n, lon_n, channels)
    key_rows = projected[:, channels : 2 * channels].reshape(lat_n, lon_n, channels)
    value_rows = projected[:, 2 * channels :].reshape(lat_n, lon_n, channels)
    query_heads = queries.reshape(lat_n, lon_n, H, head_dim)
    key_part = lax.all_gather(key_rows, "lon", axis=1, tiled=True)
    value_part = lax.all_gather(value_rows, "lon", axis=1, tiled=True)
    bias_part = lax.all_gather(key_bias, "lon", axis=1, tiled=True)
    span = key_part.shape[1]
    key_heads = key_part.reshape(lat_n, span, H, head_dim)
    value_heads = value_part.reshape(lat_n, span, H, head_dim)
    scores = (
        jnp.einsum("aqhd,akhd->ahqk", query_heads, key_heads, preferred_element_type=jnp.float32)
        * score_scale
    )
    scores = scores + jnp.transpose(bias_part, (0, 2, 1)).astype(jnp.float32)[:, :, None, :]
    weights = jnp.exp(scores - jnp.max(scores, axis=-1)[..., None])
    denom = jnp.sum(weights, axis=-1)
    accum = jnp.einsum(
        "ahqk,akhd->ahqd",
        weights.astype(jnp.bfloat16),
        value_heads,
        preferred_element_type=jnp.float32,
    )
    attended = (
        jnp.transpose(accum / denom[..., None], (0, 2, 1, 3))
        .reshape(row_count, channels)
        .astype(jnp.bfloat16)
    )
    mixed = residual.astype(jnp.float32) + jnp.dot(
        attended, out_weight, preferred_element_type=jnp.float32
    )
    return mixed.astype(jnp.bfloat16).reshape(lat_n, lon_n, channels)


VMEM = pltpu.VMEM
ANY = pl.ANY


def vspec():
    return pl.BlockSpec(memory_space=VMEM)


def sspec():
    return pl.BlockSpec(memory_space=pltpu.SMEM)


def aspec():
    return pl.BlockSpec(memory_space=ANY)


def vout(shape, dtype):
    return VMEM(shape, dtype)


def load_kernel(pieces, *refs):
    count = (len(refs) - 1) // 2
    sem = refs[-1]
    copies = []
    for src, dst, parts in zip(refs[:count], refs[count : 2 * count], pieces):
        place = 0
        for start, size in parts:
            copy = pltpu.make_async_copy(
                src.at[pl.ds(start, size)], dst.at[pl.ds(place, size)], sem.at[len(copies)]
            )
            copy.start()
            copies.append(copy)
            place += size
    for copy in copies:
        copy.wait()


def load(arrays, ranges):
    pieces, shapes = [], []
    for a, spans in zip(arrays, ranges):
        parts = []
        for start, size in spans:
            cut = size // PIECES if size % (16 * PIECES) == 0 else size
            parts += [(start + at, cut) for at in range(0, size, cut)]
        pieces.append(tuple(parts))
        shapes.append(vout((sum(size for _, size in spans),) + a.shape[1:], a.dtype))
    total = sum(math.prod(v.shape) * 2 for v in shapes)
    return pl.pallas_call(
        functools.partial(load_kernel, tuple(pieces)),
        out_shape=tuple(shapes),
        in_specs=[aspec()] * len(arrays),
        out_specs=tuple(vspec() for _ in arrays),
        scratch_shapes=[pltpu.SemaphoreType.DMA((sum(len(p) for p in pieces),))],
        compiler_params=pltpu.CompilerParams(vmem_limit_bytes=1 << 20),
        cost_estimate=pl.CostEstimate(flops=0, bytes_accessed=total, transcendentals=0),
        name="load",
    )(*[pltpu.with_memory_space_constraint(a, pltpu.HBM) for a in arrays])


def conv_kernel(me, xa, xb, ea, eb, w, first, second, cols, ext):
    n, ch = xa.shape
    core = me[0] % 2
    odd = me[1] % 2
    if ea.shape[0] == EDGE:
        edge_a, edge_b = ea[...], eb[...]
    else:
        edge_a = ea[pl.ds(pl.multiple_of(core * (n - EDGE), 16), EDGE), :]
        edge_b = eb[pl.ds(pl.multiple_of((1 - core) * (n - EDGE), 16), EDGE), :]
    ext[pl.ds(pl.multiple_of(EDGE + core * n, 16), n), :] = xa[...]
    ext[pl.ds(pl.multiple_of(EDGE + (1 - core) * n, 16), n), :] = xb[...]
    far = EDGE + 2 * n
    ext[pl.ds(pl.multiple_of((1 - core) * far, 16), EDGE), :] = edge_a
    ext[pl.ds(pl.multiple_of(core * far, 16), EDGE), :] = edge_b
    cols[pl.ds(pl.multiple_of(core * n, 16), n), ch : 2 * ch] = xa[...]
    cols[pl.ds(pl.multiple_of((1 - core) * n, 16), n), ch : 2 * ch] = xb[...]
    for b in (0, 2):
        cols[:, b * ch : (b + 1) * ch] = ext[EDGE - 1 + b : EDGE - 1 + b + 2 * n, :]
    for a, out in ((odd, first), (1 - odd, second)):
        taps = w[pl.ds(pl.multiple_of(a * 3 * ch, 16), 3 * ch), :]
        out[...] = jnp.dot(cols[...], taps, preferred_element_type=F32).astype(out.dtype)


def conv_sides(me, xa, xb, ea, eb, w):
    n, ch = xa.shape
    width = w.shape[1]
    return pl.pallas_call(
        conv_kernel,
        out_shape=(
            vout((2 * n, width), BF16),
            vout((2 * n, width), BF16),
            vout((2 * n, 3 * ch), BF16),
        ),
        in_specs=[sspec()] + [vspec()] * 5,
        out_specs=(vspec(),) * 3,
        scratch_shapes=[VMEM((2 * n + 2 * EDGE, ch), BF16)],
        compiler_params=pltpu.CompilerParams(vmem_limit_bytes=6 << 20),
        cost_estimate=pl.CostEstimate(
            flops=2 * 2 * n * 6 * ch * width, bytes_accessed=2 * 6 * ch * width, transcendentals=0
        ),
        name="conv_sides",
    )(me, xa, xb, ea, eb, w)


def middle_kernel(me, cols, w, mid, own, valid):
    lane = me[0]
    ch = cols.shape[1] // 3
    width = mid.shape[1]
    mid[...] = jnp.dot(cols[...], w[...], preferred_element_type=F32)
    own[...] = cols[:, pl.ds(pl.multiple_of(ch + lane * width, width), width)].astype(F32)
    inner = jnp.logical_and(me[1] > 0, me[1] < me[2] - 1)
    valid[...] = jnp.where(inner, jnp.ones(valid.shape, F32), jnp.zeros(valid.shape, F32))


def conv_middle(me, cols, w):
    rows, depth = cols.shape
    width = w.shape[1]
    return pl.pallas_call(
        middle_kernel,
        out_shape=(
            vout((rows, width), F32),
            vout((rows, width), F32),
            vout((1, width), F32),
        ),
        in_specs=[sspec(), vspec(), vspec()],
        out_specs=(vspec(),) * 3,
        compiler_params=pltpu.CompilerParams(vmem_limit_bytes=4 << 20),
        cost_estimate=pl.CostEstimate(
            flops=2 * rows * depth * width, bytes_accessed=2 * depth * width, transcendentals=0
        ),
        name="conv_middle",
    )(me, cols, w)


def residual_of(first, second, mid, own, valid):
    south = jnp.where(valid > 0.5, second.astype(F32), 0.0)
    conv_out = (first.astype(F32) + south + mid).astype(BF16)
    return (own + conv_out.astype(F32)).astype(BF16)


def joined_kernel(first, second, mid, own, valid, bias, out):
    rows = mid.shape[0]
    out[0:rows, :] = residual_of(
        first[...], second[...], mid[...], own[...], valid[...]
    )
    out[rows : rows + H, :] = bias[...]


def joined_residual(first, second, mid, own, valid, bias):
    rows, width = mid.shape
    return pl.pallas_call(
        joined_kernel,
        out_shape=vout((rows + H, width), BF16),
        in_specs=[vspec()] * 6,
        out_specs=vspec(),
        compiler_params=pltpu.CompilerParams(vmem_limit_bytes=2 << 20),
        cost_estimate=pl.CostEstimate(
            flops=4 * rows * width, bytes_accessed=8 * rows * width, transcendentals=0
        ),
        name="joined_residual",
    )(first, second, mid, own, valid, bias)


def factor_of(blocks, at, count, ch):
    square = 0.0
    for b in blocks:
        stream = b[pl.ds(at, count), :].astype(F32)
        square = square + jnp.sum(stream * stream, axis=-1, keepdims=True)
    return lax.rsqrt(square * (1.0 / ch) + 1e-06)


def keys_kernel(steps, me, b0, b1, b2, b3, gain, w, key_sum, value_sum, k_out, v_out):
    lane = me[0]
    rows, ch = k_out.shape
    width = b0.shape[1]
    blocks = (b0, b1, b2, b3)
    parts = [scaled(blocks[k], gain, lane, k, rows) for k in steps]
    factor = factor_of(blocks, 0, rows, ch)
    for out, acc, first in ((k_out, key_sum, ch), (v_out, value_sum, 2 * ch)):
        total = acc[...]
        for k, part in zip(steps, parts):
            at = pl.multiple_of((lane ^ k) * width, width)
            total = total + jnp.dot(
                part, w[pl.ds(at, width), first : first + ch], preferred_element_type=F32
            )
        out[...] = (total * factor).astype(BF16)


def keys_of(me, steps, blocks, gain, w, sums):
    rows = blocks[0].shape[0]
    ch = w.shape[0]
    out = vout((rows, ch), BF16)
    return pl.pallas_call(
        functools.partial(keys_kernel, steps),
        out_shape=(out, out),
        in_specs=[sspec()] + [vspec()] * 8,
        out_specs=(vspec(), vspec()),
        compiler_params=pltpu.CompilerParams(vmem_limit_bytes=16 << 20),
        cost_estimate=pl.CostEstimate(
            flops=2 * rows * ch * ch, bytes_accessed=2 * ch * ch, transcendentals=0
        ),
        name="keys_of",
    )(me, *blocks, gain, w, *sums)


def scaled(block, gain, lane, k, rows):
    return (block[0:rows, :].astype(F32) * gain[lane ^ k]).astype(BF16)


def project_kernel(steps, count, me, gain, w, *refs):
    lane = me[0]
    blocks = refs[: len(steps)]
    olds = refs[len(steps) : -count]
    outs = refs[-count:]
    rows, ch = outs[0].shape
    n = rows // 2
    width = blocks[0].shape[1]
    own = pl.multiple_of((lane % 2) * n, 16)
    parts = [scaled(b, gain, lane, k, rows) for b, k in zip(blocks, steps)]
    owns = [
        (b[pl.ds(own, n), :].astype(F32) * gain[lane ^ k]).astype(BF16)
        for b, k in zip(blocks, steps)
    ]
    for i, out in enumerate(outs):
        first, use = ((ch, parts), (2 * ch, parts), (0, owns))[i]
        acc = olds[i][...] if olds else None
        for k, part in zip(steps, use):
            at = pl.multiple_of((lane ^ k) * width, width)
            term = jnp.dot(part, w[pl.ds(at, width), first : first + ch], preferred_element_type=F32)
            acc = term if acc is None else acc + term
        out[...] = acc.astype(out.dtype)


def project(me, steps, blocks, gain, w, n, olds=(), count=3, dtype=F32):
    rows = 2 * n
    ch, width = w.shape[0], blocks[0].shape[1]
    return pl.pallas_call(
        functools.partial(project_kernel, steps, count),
        out_shape=(vout((rows, ch), dtype), vout((rows, ch), dtype), vout((n, ch), dtype))[:count],
        in_specs=[sspec()] + [vspec()] * (2 + len(blocks) + len(olds)),
        out_specs=(vspec(),) * count,
        input_output_aliases={
            3 + len(blocks) + i: i for i, old in enumerate(olds) if old.dtype == dtype
        },
        compiler_params=pltpu.CompilerParams(vmem_limit_bytes=16 << 20),
        cost_estimate=pl.CostEstimate(
            flops=2 * (2 * rows + n) * width * len(blocks) * ch,
            bytes_accessed=6 * ch * width * len(blocks),
            transcendentals=0,
        ),
        name="project",
    )(me, gain, w, *blocks, *olds)


def attend_kernel(
    steps, me, b0, b1, b2, b3, gain, w, key_sum, value_sum, query_sum, k_far, v_far, bias_y, bias_d,
    w_out, out, keys, values, query, attended
):
    lane = me[0]
    core = lane % 2
    n, ch = out.shape
    rows = 2 * n
    width = b0.shape[1]
    hd = ch // H
    blocks = (b0, b1, b2, b3)
    own = pl.multiple_of(core * n, 16)

    for first, dst, acc, at, count in (
        (0, query, query_sum, own, n),
        (ch, keys, key_sum, 0, rows),
        (2 * ch, values, value_sum, 0, rows),
    ):
        total = acc[...].astype(F32)
        for k in steps:
            part = (blocks[k][pl.ds(at, count), :].astype(F32) * gain[lane ^ k]).astype(BF16)
            place = pl.multiple_of((lane ^ k) * width, width)
            total = total + jnp.dot(
                part, w[pl.ds(place, width), first : first + ch], preferred_element_type=F32
            )
        dst[0:count, :] = (total * factor_of(blocks, at, count, ch)).astype(BF16)
    keys[rows : 2 * rows, :] = k_far[...]
    values[rows : 2 * rows, :] = v_far[...]
    pieces = []
    for a, c in ((b0, b1), (bias_y, bias_d)):
        a, c = (v[rows : rows + H, 0:n].astype(F32) for v in (a, c))
        pieces += [jnp.where(core == 0, a, c), jnp.where(core == 0, c, a)]
    bias = jnp.concatenate(pieces, axis=1)
    group = 256 // hd
    head_of = lax.broadcasted_iota(jnp.int32, (n, 256), 1) // hd
    for g in range(ch // 256):
        cols = slice(g * 256, (g + 1) * 256)
        q = query[:, cols] * jnp.asarray(1.0 / math.sqrt(hd), BF16)
        stacked = jnp.concatenate(
            [jnp.where(head_of == t, q, jnp.zeros_like(q)) for t in range(group)], axis=0
        )
        scores = lax.dot_general(
            stacked, keys[:, cols], (((1,), (1,)), ((), ())), preferred_element_type=F32
        )
        parts, totals = [], []
        for t in range(group):
            head = g * group + t
            s = scores[t * n : (t + 1) * n] + bias[head : head + 1, :]
            e = jnp.exp(s - jnp.max(s, axis=-1, keepdims=True))
            totals.append(jnp.sum(e, axis=-1, keepdims=True))
            parts.append(e.astype(BF16))
        summed = jnp.dot(
            jnp.concatenate(parts, axis=0), values[:, cols], preferred_element_type=F32
        )
        result = jnp.zeros((n, 256), F32)
        for t in range(group):
            result = jnp.where(head_of == t, summed[t * n : (t + 1) * n] / totals[t], result)
        attended[:, cols] = result.astype(BF16)
    for k, block in enumerate(blocks):
        at = pl.multiple_of((lane ^ k) * width, width)
        mixed = block[pl.ds(own, n), :].astype(F32) + jnp.dot(
            attended[...], w_out[:, pl.ds(at, width)], preferred_element_type=F32
        )
        out[:, pl.ds(at, width)] = mixed.astype(BF16)


def attend(me, steps, blocks, gain, w, sums, k_far, v_far, bias_y, bias_d, w_out):
    rows, ch = k_far.shape
    n = rows // 2
    return pl.pallas_call(
        functools.partial(attend_kernel, steps),
        out_shape=jax.ShapeDtypeStruct((n, ch), BF16),
        in_specs=[sspec()] + [vspec()] * 14,
        out_specs=vspec(),
        scratch_shapes=[
            VMEM((2 * rows, ch), BF16),
            VMEM((2 * rows, ch), BF16),
            VMEM((n, ch), BF16),
            VMEM((n, ch), BF16),
        ],
        compiler_params=pltpu.CompilerParams(vmem_limit_bytes=32 << 20),
        cost_estimate=pl.CostEstimate(
            flops=2 * rows * ch * ch + 4 * n * 2 * rows * ch * 4,
            bytes_accessed=8 * ch * ch,
            transcendentals=n * 2 * rows * H,
        ),
        name="attend",
    )(me, *blocks, gain, w, *sums, k_far, v_far, bias_y, bias_d, w_out)


def four_shard_device(fields, conv_weight, norm_gain, qkv_weight, out_weight, key_bias):
    _, n, ch = fields.shape
    width = conv_weight.shape[1]
    lane = lax.axis_index("lon")
    core = lane % 2
    me = jnp.stack([lane, lax.axis_index("lat"), lax.axis_size("lat")]).astype(jnp.int32)
    lon_size = lax.axis_size("lon")
    lat_size = lax.axis_size("lat")

    def swap(value, bit):
        return lax.ppermute(value, "lon", [(i, i ^ bit) for i in range(lon_size)])

    def lat_swap(value, first):
        def target(i):
            j = i + 1 if (i - first) % 2 == 0 else i - 1
            return j if 0 <= j < lat_size else i

        pairs = []
        for m in range(lon_size):
            for i in range(lat_size):
                j = target(i)
                to = (m, j) if j != i else (m ^ 1, i)
                pairs.append((m * lat_size + i, to[0] * lat_size + to[1]))
        return lax.ppermute(value, ("lon", "lat"), pairs)

    x = fields.reshape(n, ch)
    edge = lax.dynamic_slice_in_dim(x, core * (n - EDGE), EDGE, axis=0)
    edge_y = swap(edge, 2)
    x_c = swap(x, 1)
    x_y = swap(x, 2)
    edge_d = swap(edge_y, 1)
    x_d = swap(x_y, 1)
    bias_own = jnp.pad(key_bias.reshape(n, H).T, ((0, 0), (0, width - n)))
    taps = 3 * ch
    x_v, side_w, mid_w = load(
        (x, conv_weight, conv_weight),
        (((0, n),), ((0, taps), (2 * taps, taps)), ((taps, taps),)),
    )
    za, zb, cols = conv_sides(me, x_v, x_c, edge_y, edge_d, side_w)
    za = lat_swap(za, 0)
    zb = lat_swap(zb, 1)
    mid, own, valid = conv_middle(me, cols, mid_w)
    near = joined_residual(za, zb, mid, own, valid, bias_own)
    near_c = swap(near, 1)
    far_y = swap(near, 2)
    far_d = swap(far_y, 1)
    za, zb, cols = conv_sides(me, x_y, x_d, x_v, x_c, side_w)
    za = lat_swap(za, 0)
    zb = lat_swap(zb, 1)
    mid, own, valid = conv_middle(me, cols, mid_w)
    far = residual_of(za, zb, mid, own, valid)
    near_y = swap(far, 2)
    far_c = swap(far, 1)
    near_d = swap(near_y, 1)

    gain = norm_gain.reshape(lon_size, 1, width)
    far_sums = project(me, (0, 1), (far, far_c), gain, qkv_weight, n, count=2)
    k_far, v_far = keys_of(
        me, (2, 3), (far, far_c, far_y, far_d), gain, qkv_weight, far_sums
    )
    sums = project(me, (0, 1), (near, near_c), gain, qkv_weight, n)
    sums = project(me, (2,), (near_y,), gain, qkv_weight, n, sums, dtype=BF16)
    out = attend(
        me, (3,), (near, near_c, near_y, near_d), gain, qkv_weight, sums, k_far, v_far, far_y,
        far_d, out_weight
    )
    return out.reshape(fields.shape)


def solution(mesh):
    def on_device(*args):
        fields, conv_weight = args[0], args[1]
        special = (
            mesh.shape["lon"] == 4
            and fields.shape[0] == 1
            and conv_weight.shape[1] % 256 == 0
            and fields.shape[1] % 32 == 0
            and fields.shape[1] <= conv_weight.shape[1]
        )
        if not special:
            return general_device(*args)
        return four_shard_device(*args)

    return jax.shard_map(
        on_device,
        mesh=mesh,
        in_specs=(
            P(("ens", "lat"), "lon", None),
            P(None, "lon"),
            P(),
            P(),
            P(),
            P("lat", "lon", None),
        ),
        out_specs=P(("ens", "lat"), "lon", None),
        check_vma=False,
    )
```

```python
import functools
import math

import jax
import jax.numpy as jnp
from jax import lax
from jax.experimental import pallas as pl
from jax.experimental.pallas import tpu as pltpu
from jax.sharding import PartitionSpec as P


H = 16
EDGE = 16
PIECES = 8
F32 = jnp.float32
BF16 = jnp.bfloat16


def extended(block, sides, width):
    for axis, dim in sides:
        count = lax.axis_size(axis)
        forward = [(i, i + 1) for i in range(count - 1)]
        backward = [(target, source) for source, target in forward]
        low = lax.ppermute(
            lax.slice_in_dim(block, block.shape[dim] - width, None, axis=dim), axis, forward
        )
        high = lax.ppermute(lax.slice_in_dim(block, 0, width, axis=dim), axis, backward)
        block = jnp.concatenate([low, block, high], axis=dim)
    return block


def tap_sum(wrapped, conv_weight, out_rows, lon_total, channels):
    out_width = conv_weight.shape[1]
    accum_cols = jnp.zeros((out_rows * lon_total, out_width), jnp.float32)
    tap_idx = 0
    for step_lat in (-1, 0, 1):
        for step_lon in (-1, 0, 1):
            shifted = wrapped[
                1 + step_lat : 1 + step_lat + out_rows, 1 + step_lon : 1 + step_lon + lon_total
            ].reshape(out_rows * lon_total, channels)
            accum_cols = accum_cols + jnp.dot(
                shifted,
                conv_weight[tap_idx * channels : (tap_idx + 1) * channels],
                preferred_element_type=jnp.float32,
            )
            tap_idx += 1
    return accum_cols.reshape(out_rows, lon_total, out_width)


def general_device(fields, conv_weight, norm_gain, qkv_weight, out_weight, key_bias):
    lat_n, lon_n, channels = fields.shape
    row_count = lat_n * lon_n
    head_dim = channels // H
    score_scale = 1.0 / math.sqrt(head_dim)
    banded = extended(fields, (("lat", 0),), 1)
    circle = lax.all_gather(banded, "lon", axis=1, tiled=True)
    lon_total = circle.shape[1]
    wrapped = jnp.concatenate([circle[:, -1:], circle, circle[:, :1]], axis=1)
    out_cols = tap_sum(wrapped, conv_weight, lat_n, lon_total, channels).astype(jnp.bfloat16)
    conv_out = lax.all_to_all(out_cols, "lon", split_axis=1, concat_axis=2, tiled=True).reshape(
        row_count, channels
    )
    residual = (
        fields.reshape(row_count, channels).astype(jnp.float32) + conv_out.astype(jnp.float32)
    ).astype(jnp.bfloat16)
    stream = residual.astype(jnp.float32)
    normed = (
        stream * lax.rsqrt(jnp.mean(stream * stream, axis=-1, keepdims=True) + 1e-06) * norm_gain
    ).astype(jnp.bfloat16)
    projected = jnp.dot(normed, qkv_weight, preferred_element_type=jnp.float32).astype(jnp.bfloat16)
    queries = projected[:, :channels].reshape(lat_n, lon_n, channels)
    key_rows = projected[:, channels : 2 * channels].reshape(lat_n, lon_n, channels)
    value_rows = projected[:, 2 * channels :].reshape(lat_n, lon_n, channels)
    query_heads = queries.reshape(lat_n, lon_n, H, head_dim)
    key_part = lax.all_gather(key_rows, "lon", axis=1, tiled=True)
    value_part = lax.all_gather(value_rows, "lon", axis=1, tiled=True)
    bias_part = lax.all_gather(key_bias, "lon", axis=1, tiled=True)
    span = key_part.shape[1]
    key_heads = key_part.reshape(lat_n, span, H, head_dim)
    value_heads = value_part.reshape(lat_n, span, H, head_dim)
    scores = (
        jnp.einsum("aqhd,akhd->ahqk", query_heads, key_heads, preferred_element_type=jnp.float32)
        * score_scale
    )
    scores = scores + jnp.transpose(bias_part, (0, 2, 1)).astype(jnp.float32)[:, :, None, :]
    weights = jnp.exp(scores - jnp.max(scores, axis=-1)[..., None])
    denom = jnp.sum(weights, axis=-1)
    accum = jnp.einsum(
        "ahqk,akhd->ahqd",
        weights.astype(jnp.bfloat16),
        value_heads,
        preferred_element_type=jnp.float32,
    )
    attended = (
        jnp.transpose(accum / denom[..., None], (0, 2, 1, 3))
        .reshape(row_count, channels)
        .astype(jnp.bfloat16)
    )
    mixed = residual.astype(jnp.float32) + jnp.dot(
        attended, out_weight, preferred_element_type=jnp.float32
    )
    return mixed.astype(jnp.bfloat16).reshape(lat_n, lon_n, channels)


VMEM = pltpu.VMEM
ANY = pl.ANY


def vspec():
    return pl.BlockSpec(memory_space=VMEM)


def sspec():
    return pl.BlockSpec(memory_space=pltpu.SMEM)


def aspec():
    return pl.BlockSpec(memory_space=ANY)


def vout(shape, dtype):
    return VMEM(shape, dtype)


def load_kernel(pieces, *refs):
    count = (len(refs) - 1) // 2
    sem = refs[-1]
    copies = []
    for src, dst, parts in zip(refs[:count], refs[count : 2 * count], pieces):
        place = 0
        for start, size in parts:
            copy = pltpu.make_async_copy(
                src.at[pl.ds(start, size)], dst.at[pl.ds(place, size)], sem.at[len(copies)]
            )
            copy.start()
            copies.append(copy)
            place += size
    for copy in copies:
        copy.wait()


def load(arrays, ranges):
    pieces, shapes = [], []
    for a, spans in zip(arrays, ranges):
        parts = []
        for start, size in spans:
            cut = size // PIECES if size % (16 * PIECES) == 0 else size
            parts += [(start + at, cut) for at in range(0, size, cut)]
        pieces.append(tuple(parts))
        shapes.append(vout((sum(size for _, size in spans),) + a.shape[1:], a.dtype))
    total = sum(math.prod(v.shape) * 2 for v in shapes)
    return pl.pallas_call(
        functools.partial(load_kernel, tuple(pieces)),
        out_shape=tuple(shapes),
        in_specs=[aspec()] * len(arrays),
        out_specs=tuple(vspec() for _ in arrays),
        scratch_shapes=[pltpu.SemaphoreType.DMA((sum(len(p) for p in pieces),))],
        compiler_params=pltpu.CompilerParams(vmem_limit_bytes=1 << 20),
        cost_estimate=pl.CostEstimate(flops=0, bytes_accessed=total, transcendentals=0),
        name="load",
    )(*[pltpu.with_memory_space_constraint(a, pltpu.HBM) for a in arrays])


def conv_kernel(me, xa, xb, ea, eb, w, first, second, cols, ext):
    n, ch = xa.shape
    core = me[0] % 2
    odd = me[1] % 2
    if ea.shape[0] == EDGE:
        edge_a, edge_b = ea[...], eb[...]
    else:
        edge_a = ea[pl.ds(pl.multiple_of(core * (n - EDGE), 16), EDGE), :]
        edge_b = eb[pl.ds(pl.multiple_of((1 - core) * (n - EDGE), 16), EDGE), :]
    ext[pl.ds(pl.multiple_of(EDGE + core * n, 16), n), :] = xa[...]
    ext[pl.ds(pl.multiple_of(EDGE + (1 - core) * n, 16), n), :] = xb[...]
    far = EDGE + 2 * n
    ext[pl.ds(pl.multiple_of((1 - core) * far, 16), EDGE), :] = edge_a
    ext[pl.ds(pl.multiple_of(core * far, 16), EDGE), :] = edge_b
    cols[pl.ds(pl.multiple_of(core * n, 16), n), ch : 2 * ch] = xa[...]
    cols[pl.ds(pl.multiple_of((1 - core) * n, 16), n), ch : 2 * ch] = xb[...]
    for b in (0, 2):
        cols[:, b * ch : (b + 1) * ch] = ext[EDGE - 1 + b : EDGE - 1 + b + 2 * n, :]
    for a, out in ((odd, first), (1 - odd, second)):
        taps = w[pl.ds(pl.multiple_of(a * 3 * ch, 16), 3 * ch), :]
        out[...] = jnp.dot(cols[...], taps, preferred_element_type=F32).astype(out.dtype)


def conv_sides(me, xa, xb, ea, eb, w):
    n, ch = xa.shape
    width = w.shape[1]
    return pl.pallas_call(
        conv_kernel,
        out_shape=(
            vout((2 * n, width), BF16),
            vout((2 * n, width), BF16),
            vout((2 * n, 3 * ch), BF16),
        ),
        in_specs=[sspec()] + [vspec()] * 5,
        out_specs=(vspec(),) * 3,
        scratch_shapes=[VMEM((2 * n + 2 * EDGE, ch), BF16)],
        compiler_params=pltpu.CompilerParams(vmem_limit_bytes=6 << 20),
        cost_estimate=pl.CostEstimate(
            flops=2 * 2 * n * 6 * ch * width, bytes_accessed=2 * 6 * ch * width, transcendentals=0
        ),
        name="conv_sides",
    )(me, xa, xb, ea, eb, w)


def middle_kernel(me, cols, w, mid, own, valid):
    lane = me[0]
    ch = cols.shape[1] // 3
    width = mid.shape[1]
    mid[...] = jnp.dot(cols[...], w[...], preferred_element_type=F32)
    own[...] = cols[:, pl.ds(pl.multiple_of(ch + lane * width, width), width)].astype(F32)
    inner = jnp.logical_and(me[1] > 0, me[1] < me[2] - 1)
    valid[...] = jnp.where(inner, jnp.ones(valid.shape, F32), jnp.zeros(valid.shape, F32))


def conv_middle(me, cols, w):
    rows, depth = cols.shape
    width = w.shape[1]
    return pl.pallas_call(
        middle_kernel,
        out_shape=(
            vout((rows, width), F32),
            vout((rows, width), F32),
            vout((1, width), F32),
        ),
        in_specs=[sspec(), vspec(), vspec()],
        out_specs=(vspec(),) * 3,
        compiler_params=pltpu.CompilerParams(vmem_limit_bytes=4 << 20),
        cost_estimate=pl.CostEstimate(
            flops=2 * rows * depth * width, bytes_accessed=2 * depth * width, transcendentals=0
        ),
        name="conv_middle",
    )(me, cols, w)


def residual_of(first, second, mid, own, valid):
    south = jnp.where(valid > 0.5, second.astype(F32), 0.0)
    conv_out = (first.astype(F32) + south + mid).astype(BF16)
    return (own + conv_out.astype(F32)).astype(BF16)


def joined_kernel(first, second, mid, own, valid, bias, out):
    rows = mid.shape[0]
    out[0:rows, :] = residual_of(
        first[...], second[...], mid[...], own[...], valid[...]
    )
    out[rows : rows + H, :] = bias[...]


def joined_residual(first, second, mid, own, valid, bias):
    rows, width = mid.shape
    return pl.pallas_call(
        joined_kernel,
        out_shape=vout((rows + H, width), BF16),
        in_specs=[vspec()] * 6,
        out_specs=vspec(),
        compiler_params=pltpu.CompilerParams(vmem_limit_bytes=2 << 20),
        cost_estimate=pl.CostEstimate(
            flops=4 * rows * width, bytes_accessed=8 * rows * width, transcendentals=0
        ),
        name="joined_residual",
    )(first, second, mid, own, valid, bias)


def factor_of(blocks, at, count, ch):
    square = 0.0
    for b in blocks:
        stream = b[pl.ds(at, count), :].astype(F32)
        square = square + jnp.sum(stream * stream, axis=-1, keepdims=True)
    return lax.rsqrt(square * (1.0 / ch) + 1e-06)


def keys_kernel(steps, me, b0, b1, b2, b3, gain, w, key_sum, value_sum, k_out, v_out):
    lane = me[0]
    rows, ch = k_out.shape
    width = b0.shape[1]
    blocks = (b0, b1, b2, b3)
    parts = [scaled(blocks[k], gain, lane, k, rows) for k in steps]
    factor = factor_of(blocks, 0, rows, ch)
    for out, acc, first in ((k_out, key_sum, ch), (v_out, value_sum, 2 * ch)):
        total = acc[...].astype(F32)
        for k, part in zip(steps, parts):
            at = pl.multiple_of((lane ^ k) * width, width)
            total = total + jnp.dot(
                part, w[pl.ds(at, width), first : first + ch], preferred_element_type=F32
            )
        out[...] = (total * factor).astype(BF16)


def keys_of(me, steps, blocks, gain, w, sums):
    rows = blocks[0].shape[0]
    ch = w.shape[0]
    out = vout((rows, ch), BF16)
    return pl.pallas_call(
        functools.partial(keys_kernel, steps),
        out_shape=(out, out),
        in_specs=[sspec()] + [vspec()] * 8,
        out_specs=(vspec(), vspec()),
        compiler_params=pltpu.CompilerParams(vmem_limit_bytes=16 << 20),
        cost_estimate=pl.CostEstimate(
            flops=2 * rows * ch * ch, bytes_accessed=2 * ch * ch, transcendentals=0
        ),
        name="keys_of",
    )(me, *blocks, gain, w, *sums)


def scaled(block, gain, lane, k, rows):
    return (block[0:rows, :].astype(F32) * gain[lane ^ k]).astype(BF16)


def project_kernel(steps, count, me, gain, w, *refs):
    lane = me[0]
    blocks = refs[: len(steps)]
    olds = refs[len(steps) : -count]
    outs = refs[-count:]
    rows, ch = outs[0].shape
    n = rows // 2
    width = blocks[0].shape[1]
    own = pl.multiple_of((lane % 2) * n, 16)
    parts = [scaled(b, gain, lane, k, rows) for b, k in zip(blocks, steps)]
    owns = [
        (b[pl.ds(own, n), :].astype(F32) * gain[lane ^ k]).astype(BF16)
        for b, k in zip(blocks, steps)
    ]
    for i, out in enumerate(outs):
        first, use = ((ch, parts), (2 * ch, parts), (0, owns))[i]
        acc = olds[i][...].astype(F32) if olds else None
        for k, part in zip(steps, use):
            at = pl.multiple_of((lane ^ k) * width, width)
            term = jnp.dot(part, w[pl.ds(at, width), first : first + ch], preferred_element_type=F32)
            acc = term if acc is None else acc + term
        out[...] = acc.astype(out.dtype)


def project(me, steps, blocks, gain, w, n, olds=(), count=3, dtype=F32):
    rows = 2 * n
    ch, width = w.shape[0], blocks[0].shape[1]
    return pl.pallas_call(
        functools.partial(project_kernel, steps, count),
        out_shape=(vout((rows, ch), dtype), vout((rows, ch), dtype), vout((n, ch), dtype))[:count],
        in_specs=[sspec()] + [vspec()] * (2 + len(blocks) + len(olds)),
        out_specs=(vspec(),) * count,
        input_output_aliases={
            3 + len(blocks) + i: i for i, old in enumerate(olds) if old.dtype == dtype
        },
        compiler_params=pltpu.CompilerParams(vmem_limit_bytes=16 << 20),
        cost_estimate=pl.CostEstimate(
            flops=2 * (2 * rows + n) * width * len(blocks) * ch,
            bytes_accessed=6 * ch * width * len(blocks),
            transcendentals=0,
        ),
        name="project",
    )(me, gain, w, *blocks, *olds)


def attend_kernel(
    steps, me, b0, b1, b2, b3, gain, w, key_sum, value_sum, query_sum, k_far, v_far, bias_y, bias_d,
    w_out, out, keys, values, query, attended
):
    lane = me[0]
    core = lane % 2
    n, ch = out.shape
    rows = 2 * n
    width = b0.shape[1]
    hd = ch // H
    blocks = (b0, b1, b2, b3)
    own = pl.multiple_of(core * n, 16)

    for first, dst, acc, at, count in (
        (0, query, query_sum, own, n),
        (ch, keys, key_sum, 0, rows),
        (2 * ch, values, value_sum, 0, rows),
    ):
        total = acc[...].astype(F32)
        for k in steps:
            part = (blocks[k][pl.ds(at, count), :].astype(F32) * gain[lane ^ k]).astype(BF16)
            place = pl.multiple_of((lane ^ k) * width, width)
            total = total + jnp.dot(
                part, w[pl.ds(place, width), first : first + ch], preferred_element_type=F32
            )
        dst[0:count, :] = (total * factor_of(blocks, at, count, ch)).astype(BF16)
    keys[rows : 2 * rows, :] = k_far[...]
    values[rows : 2 * rows, :] = v_far[...]
    pieces = []
    for a, c in ((b0, b1), (bias_y, bias_d)):
        a, c = (v[rows : rows + H, 0:n].astype(F32) for v in (a, c))
        pieces += [jnp.where(core == 0, a, c), jnp.where(core == 0, c, a)]
    bias = jnp.concatenate(pieces, axis=1)
    group = 256 // hd
    head_of = lax.broadcasted_iota(jnp.int32, (n, 256), 1) // hd
    for g in range(ch // 256):
        cols = slice(g * 256, (g + 1) * 256)
        q = query[:, cols] * jnp.asarray(1.0 / math.sqrt(hd), BF16)
        stacked = jnp.concatenate(
            [jnp.where(head_of == t, q, jnp.zeros_like(q)) for t in range(group)], axis=0
        )
        scores = lax.dot_general(
            stacked, keys[:, cols], (((1,), (1,)), ((), ())), preferred_element_type=F32
        )
        parts, totals = [], []
        for t in range(group):
            head = g * group + t
            s = scores[t * n : (t + 1) * n] + bias[head : head + 1, :]
            e = jnp.exp(s - jnp.max(s, axis=-1, keepdims=True))
            totals.append(jnp.sum(e, axis=-1, keepdims=True))
            parts.append(e.astype(BF16))
        summed = jnp.dot(
            jnp.concatenate(parts, axis=0), values[:, cols], preferred_element_type=F32
        )
        result = jnp.zeros((n, 256), F32)
        for t in range(group):
            result = jnp.where(head_of == t, summed[t * n : (t + 1) * n] / totals[t], result)
        attended[:, cols] = result.astype(BF16)
    for k, block in enumerate(blocks):
        at = pl.multiple_of((lane ^ k) * width, width)
        mixed = block[pl.ds(own, n), :].astype(F32) + jnp.dot(
            attended[...], w_out[:, pl.ds(at, width)], preferred_element_type=F32
        )
        out[:, pl.ds(at, width)] = mixed.astype(BF16)


def attend(me, steps, blocks, gain, w, sums, k_far, v_far, bias_y, bias_d, w_out):
    rows, ch = k_far.shape
    n = rows // 2
    return pl.pallas_call(
        functools.partial(attend_kernel, steps),
        out_shape=jax.ShapeDtypeStruct((n, ch), BF16),
        in_specs=[sspec()] + [vspec()] * 14,
        out_specs=vspec(),
        scratch_shapes=[
            VMEM((2 * rows, ch), BF16),
            VMEM((2 * rows, ch), BF16),
            VMEM((n, ch), BF16),
            VMEM((n, ch), BF16),
        ],
        compiler_params=pltpu.CompilerParams(vmem_limit_bytes=32 << 20),
        cost_estimate=pl.CostEstimate(
            flops=2 * rows * ch * ch + 4 * n * 2 * rows * ch * 4,
            bytes_accessed=8 * ch * ch,
            transcendentals=n * 2 * rows * H,
        ),
        name="attend",
    )(me, *blocks, gain, w, *sums, k_far, v_far, bias_y, bias_d, w_out)


def four_shard_device(fields, conv_weight, norm_gain, qkv_weight, out_weight, key_bias):
    _, n, ch = fields.shape
    width = conv_weight.shape[1]
    lane = lax.axis_index("lon")
    core = lane % 2
    me = jnp.stack([lane, lax.axis_index("lat"), lax.axis_size("lat")]).astype(jnp.int32)
    lon_size = lax.axis_size("lon")
    lat_size = lax.axis_size("lat")

    def swap(value, bit):
        return lax.ppermute(value, "lon", [(i, i ^ bit) for i in range(lon_size)])

    def lat_swap(value, first):
        def target(i):
            j = i + 1 if (i - first) % 2 == 0 else i - 1
            return j if 0 <= j < lat_size else i

        pairs = []
        for m in range(lon_size):
            for i in range(lat_size):
                j = target(i)
                to = (m, j) if j != i else (m ^ 1, i)
                pairs.append((m * lat_size + i, to[0] * lat_size + to[1]))
        return lax.ppermute(value, ("lon", "lat"), pairs)

    x = fields.reshape(n, ch)
    edge = lax.dynamic_slice_in_dim(x, core * (n - EDGE), EDGE, axis=0)
    edge_y = swap(edge, 2)
    x_c = swap(x, 1)
    x_y = swap(x, 2)
    edge_d = swap(edge_y, 1)
    x_d = swap(x_y, 1)
    bias_own = jnp.pad(key_bias.reshape(n, H).T, ((0, 0), (0, width - n)))
    taps = 3 * ch
    x_v, side_w, mid_w = load(
        (x, conv_weight, conv_weight),
        (((0, n),), ((0, taps), (2 * taps, taps)), ((taps, taps),)),
    )
    za, zb, cols = conv_sides(me, x_v, x_c, edge_y, edge_d, side_w)
    za = lat_swap(za, 0)
    zb = lat_swap(zb, 1)
    mid, own, valid = conv_middle(me, cols, mid_w)
    near = joined_residual(za, zb, mid, own, valid, bias_own)
    near_c = swap(near, 1)
    far_y = swap(near, 2)
    far_d = swap(far_y, 1)
    za, zb, cols = conv_sides(me, x_y, x_d, x_v, x_c, side_w)
    za = lat_swap(za, 0)
    zb = lat_swap(zb, 1)
    mid, own, valid = conv_middle(me, cols, mid_w)
    far = residual_of(za, zb, mid, own, valid)
    near_y = swap(far, 2)
    far_c = swap(far, 1)
    near_d = swap(near_y, 1)

    gain = norm_gain.reshape(lon_size, 1, width)
    far_sums = project(me, (0, 1), (far, far_c), gain, qkv_weight, n, count=2, dtype=BF16)
    k_far, v_far = keys_of(
        me, (2, 3), (far, far_c, far_y, far_d), gain, qkv_weight, far_sums
    )
    sums = project(me, (0, 1), (near, near_c), gain, qkv_weight, n, dtype=BF16)
    sums = project(me, (2,), (near_y,), gain, qkv_weight, n, sums, dtype=BF16)
    out = attend(
        me, (3,), (near, near_c, near_y, near_d), gain, qkv_weight, sums, k_far, v_far, far_y,
        far_d, out_weight
    )
    return out.reshape(fields.shape)


def solution(mesh):
    def on_device(*args):
        fields, conv_weight = args[0], args[1]
        special = (
            mesh.shape["lon"] == 4
            and fields.shape[0] == 1
            and conv_weight.shape[1] % 256 == 0
            and fields.shape[1] % 32 == 0
            and fields.shape[1] <= conv_weight.shape[1]
        )
        if not special:
            return general_device(*args)
        return four_shard_device(*args)

    return jax.shard_map(
        on_device,
        mesh=mesh,
        in_specs=(
            P(("ens", "lat"), "lon", None),
            P(None, "lon"),
            P(),
            P(),
            P(),
            P("lat", "lon", None),
        ),
        out_specs=P(("ens", "lat"), "lon", None),
        check_vma=False,
    )
```
